32 devices in a mesh: species: 4 (over z), wave: 8 (over y, x, core).
Axes of the slice: x: 2, y: 2, z: 4, core: 2. Of those that a mesh axis runs over, the one named last changes fastest.
Arguments:
- dest_tiles: int32 [4, 256, 1], P('species', 'wave'), may hold values from 0 to 7; in each aligned block of 32 rows (0 to 31, 32 to 63, ..., all dimensions but the last counted through in order) at most 8 rows name the same one
- line_counts: int32 [4, 256], P('species', 'wave'), may hold values from 32 to 128
- wing_widths: int32 [4, 256], P('species', 'wave'), may hold values from 16 to 64
- species_ids: int32 [4, 32768], P('species', 'wave'), may hold values from 0 to 3
- offsets: float32 [4, 32768], P('species', 'wave'), may hold values from 0 to 256
- strengths: float32 [4, 32768], P('species', 'wave'), may hold values from 0.01 to 0.2
- doppler: float32 [4, 32768], P('species', 'wave'), may hold values from 0.5 to 6
- lorentz: float32 [4, 32768], P('species', 'wave'), may hold values from 0.1 to 4
- energy: float32 [4, 32768], P('species', 'wave'), may hold values from 0.05 to 3
- temp_scale: float32 [16], replicated, may hold values from 0.5 to 2
- press_scale: float32 [16], replicated, may hold values from 0.2 to 4
- inverse_temp: float32 [16], replicated, may hold values from 0.2 to 1.5
- abundances: float32 [4, 4, 4, 16], P(None, 'species'), may hold values from 0.05 to 1
Outputs:
- opacity: float32 [4, 16, 2048], P(None, 'species', 'wave')
The draws below stay inside these ranges and needn't reach their ends.
Inputs may be any that keep to these rules, and one draw needn't show every extreme that they name: `dest_tiles`: within one device's 32 blocks no tile is named more than 8 times.
All inputs are finite; a program needn't handle non-finite values.
Results may differ from the reference program's by a relative error of at most 0.0004.
Values sent between devices are 32-bit elements; how exact they have to be, the bound alone decides.
A program may use at most 64 MiB of HBM per device.

```python
import math
import jax
import jax.numpy as jnp
import numpy as np
from jax import lax

WAVE_DEV = 256
TP = 16
MIXES = 4
SUB = 4
HALO = 64
BLOCKS_DEV = 32
MOST = 8
GROUPS = 4
LINES = 32768
BLOCKS = 256
NWAVE = 2048
N_SPECIES = 4
N_WAVE = 8


def place_ends(values, stream_key, low, top_value):
    longest = values.shape.index(max(values.shape))
    spots = []
    for shift in (0, 1):
        where = [jax.random.randint(jax.random.fold_in(stream_key, axis), (), 0, length) for axis, length in enumerate(values.shape)]
        where[longest] = (where[longest] + shift) % values.shape[longest]
        spots.append(tuple(where))
    return values.at[spots[0]].set(low).at[spots[1]].set(top_value)


def shard_levels(rng, shape, split, smallest, high):
    factor_of = 1.0
    for axis_at, parts in split:
        heights = jax.random.uniform(jax.random.fold_in(jax.random.fold_in(rng, 6), axis_at), (parts,), jnp.float32, smallest / len(split), high / len(split))
        factor_of = factor_of * jnp.repeat(jnp.exp(heights), shape[axis_at] // parts).reshape((-1,) + (1,) * (len(shape) - 1 - axis_at))
    return factor_of


def assign_block(own_key, own, number, rows, amount, top, bound, skew):
    sequence = jax.random.permutation(own_key, amount)
    packed, ordinary = portions_of(amount, rows * top, bound, skew, True), portions_of(amount, rows * top, bound, skew, False)
    places = jnp.arange(amount)

    def named(sizes, turn):
        used = int((sizes > 0).sum())
        fixed = max(1, used // 4)
        moved = fixed + (places - fixed + turn * (used - fixed)) % max(1, amount - fixed)
        return jnp.zeros((amount,), jnp.int32).at[sequence[jnp.where(places < fixed, places, moved)]].set(jnp.asarray(sizes, jnp.int32))

    sizes = jnp.where(number % 4 == 0, named(packed, number // 4), named(ordinary, number - number // 4 - 1))
    mixed = jax.random.permutation(jax.random.fold_in(own, 3), amount)
    giver, sink = mixed[0:amount // 2 * 2:2], mixed[1:amount // 2 * 2:2]
    margin = jnp.minimum(sizes[giver] - 1, bound - sizes[sink]) // 2
    margin = jnp.where((giver == sequence[0]) | (sink == sequence[0]) | (sizes[sink] == 0), 0, jnp.maximum(margin, 0))
    moved = jax.random.randint(jax.random.fold_in(own, 4), (amount // 2,), 0, 1 << 20) % (margin + 1)
    sizes = sizes.at[giver].add(-moved).at[sink].add(moved)
    items = jnp.searchsorted(jnp.cumsum(sizes), jnp.arange(rows * top), side="right").astype(jnp.int32)
    table = items.reshape(top, rows).T
    table = table[jax.random.permutation(jax.random.fold_in(own, 1), rows)]
    turn = jax.random.randint(jax.random.fold_in(own, 2), (rows, 1), 0, top)
    return jnp.take_along_axis(table, (jnp.arange(top)[None, :] + turn) % top, axis=1)


def portions_of(amount, total, limit, skew, full):
    weights = [(1 << 20) // math.isqrt(standing ** skew) + 1 for standing in range(1, amount + 1)]
    largest = limit if full else min(limit, max(-(-total // amount), total * weights[0] // sum(weights)))
    least = 1 if total - largest >= amount - 1 else 0
    holding, spare = [largest] + [least] * (amount - 1), total - largest - least * (amount - 1)
    while spare > 0:
        free = [i for i in range(1, amount) if holding[i] < largest] or [i for i in range(1, amount) if holding[i] < limit]
        whole, left = sum([weights[i] for i in free]), spare
        for i in free:
            extra = min(limit - holding[i], max(1, left * weights[i] // whole), spare)
            holding[i] = holding[i] + extra
            spare = spare - extra
    return np.array(holding)


def setup_inputs(seed: int = 0) -> dict:
    key_of = jax.random.split(jax.random.key(seed), 14)
    dest_tiles_keys = jax.random.split(jax.random.fold_in(key_of[0], 1), GROUPS * BLOCKS // BLOCKS_DEV)
    dest_tiles_turns = jax.random.permutation(jax.random.fold_in(key_of[0], 3), GROUPS * BLOCKS // BLOCKS_DEV)
    dest_tiles = jax.vmap(lambda own, number: assign_block(jax.random.fold_in(key_of[0], 2), own, number, BLOCKS_DEV, N_WAVE, 1, MOST, 2))(dest_tiles_keys, dest_tiles_turns).reshape((GROUPS, BLOCKS, 1))
    line_counts = place_ends(jax.random.randint(key_of[1], (GROUPS, BLOCKS), 32, 129), jax.random.fold_in(key_of[1], 1), 32, 128).astype(jnp.int32)
    wing_widths = place_ends(jax.random.randint(key_of[2], (GROUPS, BLOCKS), HALO // 4, HALO + 1), jax.random.fold_in(key_of[2], 1), HALO // 4, HALO).astype(jnp.int32)
    species_ids = place_ends(jax.random.randint(key_of[3], (GROUPS, LINES), 0, SUB), jax.random.fold_in(key_of[3], 1), 0, SUB - 1).astype(jnp.int32)
    offsets = jnp.clip(256.0 * jax.random.uniform(key_of[4], (GROUPS, LINES), jnp.float32) ** shard_levels(key_of[4], (GROUPS, LINES), ((0, 4), (1, 8)), -0.2, 0.2), 0.0, 256.0)
    strengths = jnp.clip(jnp.exp(math.log(0.2) - 2.9957323 * jax.random.uniform(key_of[5], (GROUPS, LINES), jnp.float32) ** shard_levels(key_of[5], (GROUPS, LINES), ((0, 4), (1, 8)), -0.2, 0.2)), 0.01, 0.2)
    doppler = jnp.clip(jnp.exp(math.log(6.0) - 2.4849066 * jax.random.uniform(key_of[6], (GROUPS, LINES), jnp.float32) ** shard_levels(key_of[6], (GROUPS, LINES), ((0, 4), (1, 8)), -0.2, 0.2)), 0.5, 6.0)
    lorentz = jnp.clip(jnp.exp(math.log(4.0) - 3.6888794 * jax.random.uniform(key_of[7], (GROUPS, LINES), jnp.float32) ** shard_levels(key_of[7], (GROUPS, LINES), ((0, 4), (1, 8)), -0.2, 0.2)), 0.1, 4.0)
    energy = jnp.clip(jnp.exp(math.log(3.0) - 4.0943445 * jax.random.uniform(key_of[8], (GROUPS, LINES), jnp.float32) ** shard_levels(key_of[8], (GROUPS, LINES), ((0, 4), (1, 8)), -0.2, 0.2)), 0.05, 3.0)
    temp_scale = jnp.clip(jnp.exp(jax.random.uniform(key_of[9], (TP,), jnp.float32, math.log(0.5), math.log(2.0))), 0.5, 2.0)
    press_scale = jnp.clip(jnp.exp(jax.random.uniform(key_of[10], (TP,), jnp.float32, math.log(0.2), math.log(4.0))), 0.2, 4.0)
    inverse_temp = jnp.clip(jax.random.uniform(key_of[11], (TP,), jnp.float32, 0.2, 1.5), 0.2, 1.5)
    abundances = jnp.clip(jnp.exp(math.log(1.0) - 2.9957323 * jax.random.uniform(key_of[12], (MIXES, GROUPS, SUB, TP), jnp.float32) ** shard_levels(key_of[12], (MIXES, GROUPS, SUB, TP), ((1, 4),), -0.2, 0.2)), 0.05, 1.0)
    return {"dest_tiles": dest_tiles, "line_counts": line_counts, "wing_widths": wing_widths, "species_ids": species_ids, "offsets": offsets, "strengths": strengths, "doppler": doppler, "lorentz": lorentz, "energy": energy, "temp_scale": temp_scale, "press_scale": press_scale, "inverse_temp": inverse_temp, "abundances": abundances}


def profile(center, doppler_row, lorentz_row, wing_reach, temp_scale, press_scale, extent):
    doppler_width = temp_scale[:, None] * doppler_row[None, :]
    pressure_width = press_scale[:, None] * lorentz_row[None, :]
    gauss_full = 2.35482 * doppler_width
    lorentz_full = 2.0 * pressure_width
    voigt_width = (gauss_full ** 5 + 2.69269 * gauss_full ** 4 * lorentz_full
                   + 2.42843 * gauss_full ** 3 * lorentz_full ** 2
                   + 4.47163 * gauss_full ** 2 * lorentz_full ** 3
                   + 0.07842 * gauss_full * lorentz_full ** 4 + lorentz_full ** 5) ** 0.2
    lorentz_ratio = lorentz_full / voigt_width
    mixing = 1.36603 * lorentz_ratio - 0.47719 * lorentz_ratio * lorentz_ratio + 0.11116 * lorentz_ratio * lorentz_ratio * lorentz_ratio
    points = jnp.arange(extent).astype(jnp.float32) - HALO
    offset = points[None, None, :] - center[None, :, None]
    square = offset * offset
    voigt_col = voigt_width[:, :, None]
    gauss_shape = (0.9394373 / voigt_col) * jnp.exp(-2.7725887 * square / (voigt_col * voigt_col))
    lorentz_shape = (0.15915494 * voigt_col) / (square + 0.25 * voigt_col * voigt_col)
    mix_col = mixing[:, :, None]
    profile_values = mix_col * lorentz_shape + (1.0 - mix_col) * gauss_shape
    return jnp.where(jnp.abs(offset) <= wing_reach[None, :, None], profile_values, 0.0)


def mix_weights(abund_group, per_species, energy_row, inverse_temp):
    boltzmann = jnp.exp(-inverse_temp[:, None] * energy_row[None, :])
    summed = jnp.sum(abund_group[:, :, :, None] * per_species[None, :, None, :], axis=1)
    return summed * boltzmann[None]


def regroup(array):
    return array.reshape((array.shape[0] // 8, 8) + array.shape[1:])


def reference(dest_tiles, line_counts, wing_widths, species_ids, offsets, strengths, doppler, lorentz, energy, temp_scale, press_scale, inverse_temp, abundances):
    nblocks = BLOCKS_DEV * N_WAVE
    extent = WAVE_DEV + 2 * HALO
    lanes = jnp.arange(128)
    kinds = jnp.arange(SUB)
    canvas = jnp.zeros((MIXES, TP, NWAVE + 2 * HALO), jnp.float32)
    for group in range(N_SPECIES):
        live = lanes[None, :] < line_counts[group][:, None]
        kind_rows = species_ids[group].reshape(nblocks, 128)
        base = jnp.where(live, strengths[group].reshape(nblocks, 128), 0.0)
        per_species = jnp.where(kind_rows[:, None, :] == kinds[None, :, None], base[:, None, :], 0.0)
        fields = (dest_tiles[group, :, 0], wing_widths[group].astype(jnp.float32),
                  offsets[group].reshape(nblocks, 128), doppler[group].reshape(nblocks, 128),
                  lorentz[group].reshape(nblocks, 128), energy[group].reshape(nblocks, 128), per_species)
        batched = jax.tree.map(regroup, fields)
        abund_group = abundances[:, group]

        def advance(canvas, item):
            tiles, reach, center, dop_rows, lor_rows, energy_rows, strength_rows = item
            for slot in range(8):
                reach_row = jnp.broadcast_to(reach[slot], (128,))
                values = profile(center[slot], dop_rows[slot], lor_rows[slot], reach_row, temp_scale, press_scale, extent).astype(jnp.bfloat16)
                weights = mix_weights(abund_group, strength_rows[slot], energy_rows[slot], inverse_temp).astype(jnp.bfloat16)
                part = jnp.einsum("mtl,tln->mtn", weights.astype(jnp.float32), values.astype(jnp.float32), precision=lax.Precision.HIGHEST)
                start = (tiles[slot] * WAVE_DEV).astype(jnp.int32)
                zero = jnp.zeros((), jnp.int32)
                window = lax.dynamic_slice(canvas, (zero, zero, start), (MIXES, TP, extent))
                canvas = lax.dynamic_update_slice(canvas, window + part, (zero, zero, start))
            return canvas, None

        canvas = lax.scan(advance, canvas, batched)[0]
    return canvas[:, :, HALO:HALO + NWAVE]
```

```python
import functools

import jax
import jax.numpy as jnp
from jax import lax
from jax.experimental import pallas as pl
from jax.experimental.pallas import tpu as pltpu
from jax.sharding import PartitionSpec as P

LANES = 128
HALO = 64
STEP = 16
WINDOW = LANES + STEP
QUARTER = 64
SPAN = QUARTER + 2 * HALO
STAGES = 2
FAR = 1e37
MESH = pl.DeviceIdType.MESH


def column(ref, count):
    rows = lax.broadcasted_iota(jnp.int32, (count, LANES), 0)
    out = jnp.zeros((count, LANES), jnp.float32)
    for index in range(count):
        out = jnp.where(rows == index, ref[index], out)
    return out


def kernel(
    sizes,
    tiles,
    counts,
    wings,
    temp,
    press,
    inverse,
    abund,
    kinds,
    offsets,
    strengths,
    doppler,
    lorentz,
    energy,
    out,
    square,
    decay,
    lor_amp,
    gau_amp,
    table,
    bits,
    route,
    coef,
    accum,
    edge,
    send,
    recv,
    zsend,
    zrecv,
    send_sem,
    recv_sem,
    zsend_sem,
    zrecv_sem,
):
    nspecies, nwave, nblocks, points, mixes, sub = sizes
    chunk = points // nspecies
    last = nspecies - 1
    rows = 2 * mixes
    total_rows = nwave * rows
    me_s = lax.axis_index("species")
    me_w = lax.axis_index("wave")

    barrier = pltpu.get_barrier_semaphore()
    for step in range(1, nwave):
        pl.semaphore_signal(
            barrier,
            inc=1,
            device_id=(me_s, lax.rem(me_w + step, nwave)),
            device_id_type=MESH,
        )
    for step in range(1, nspecies):
        pl.semaphore_signal(
            barrier,
            inc=1,
            device_id=(lax.rem(me_s + step, nspecies), me_w),
            device_id_type=MESH,
        )

    temp_col = column(temp, points)
    press_col = column(press, points)
    inverse_col = column(inverse, points)
    lane_row = lax.broadcasted_iota(jnp.int32, (1, LANES), 1)
    local = lax.broadcasted_iota(jnp.int32, (WINDOW, LANES), 0).astype(jnp.float32) - HALO
    row_point = lax.broadcasted_iota(jnp.int32, (points, LANES), 0)
    row8 = lax.broadcasted_iota(jnp.int32, (rows, LANES), 0)
    row_half = lax.div(row8, mixes)
    for mix in range(mixes):
        for kind in range(sub):
            value = jnp.zeros((points, LANES), jnp.float32)
            for point in range(points):
                value = jnp.where(row_point == point, abund[mix, 0, kind, point], value)
            coef[mix, kind] = value

    def prepare(block, carry):
        here = pl.ds(pl.multiple_of(block * LANES, LANES), LANES)
        center = offsets[:, here]
        quarter = jnp.clip(jnp.floor(center * (1.0 / QUARTER)), 0.0, 3.0)
        center = center - quarter * float(QUARTER)
        hop = jnp.clip(jnp.floor(center * (1.0 / STEP)), 0.0, float(QUARTER // STEP - 1))
        reach = wings[0, block].astype(jnp.float32)
        offset = (local + hop * float(STEP)) - center
        sq = offset * offset
        square[:, here] = jnp.where(sq <= reach * reach, sq, FAR)
        hop_int = hop.astype(jnp.int32)
        for stage in range(STAGES):
            bit = (hop_int >> stage) & 1
            bits[block, stage] = jnp.broadcast_to(bit.astype(jnp.float32), (STEP, LANES))
        gauss = 2.35482 * (temp_col * doppler[:, here])
        lor = 2.0 * (press_col * lorentz[:, here])
        g2 = gauss * gauss
        g4 = g2 * g2
        l2 = lor * lor
        l4 = l2 * l2
        poly = (
            g4 * gauss
            + 2.69269 * g4 * lor
            + 2.42843 * (g2 * gauss) * l2
            + 4.47163 * g2 * (l2 * lor)
            + 0.07842 * gauss * l4
            + l4 * lor
        )
        width = jnp.exp(0.2 * jnp.log(poly))
        inv = 1.0 / width
        ratio = lor * inv
        eta = ratio * (1.36603 + ratio * (-0.47719 + ratio * 0.11116))
        decay[block] = -4.0 * (inv * inv)
        lor_amp[block] = eta * inv * (4.0 * 0.15915494)
        gau_amp[block] = (1.0 - eta) * inv * 0.9394373
        boltz = jnp.exp(-(inverse_col * energy[:, here]))
        strength = jnp.where(lane_row < counts[0, block], strengths[:, here], 0.0)
        kind_row = kinds[:, here]
        for mix in range(mixes):
            mixed = coef[mix, 0]
            for kind in range(1, sub):
                mixed = jnp.where(kind_row == kind, coef[mix, kind], mixed)
            mixed = (mixed * strength) * boltz
            for half in range(2):
                table[block, pl.ds(half * mixes + mix, points, stride=rows), :] = mixed
        target = tiles[0, block]
        for parity in range(2):
            chosen = jnp.where((2 * row_half + parity).astype(jnp.float32) == quarter, 1.0, 0.0)
            for tile in range(0, nwave, 2):
                pair = jnp.concatenate(
                    [jnp.where(target == tile, chosen, 0.0), jnp.where(target == tile + 1, chosen, 0.0)],
                    axis=0,
                )
                route[block, pl.ds(parity * total_rows + tile * rows, 2 * rows), :] = pair.astype(jnp.bfloat16)
        return carry

    lax.fori_loop(0, nblocks, prepare, 0, unroll=4)

    accum[...] = jnp.zeros(accum.shape, jnp.float32)
    edge[...] = jnp.zeros(edge.shape, jnp.float32)
    low_lane = lax.broadcasted_iota(jnp.int32, (total_rows, LANES), 1) < QUARTER

    def group_of(phase):
        return lax.rem(me_s + 1 + phase, nspecies)

    def evaluate(phase, inner):
        point = group_of(phase) * chunk + inner
        weights = []
        profiles = []
        for block in range(nblocks):
            here = pl.ds(block * LANES, LANES)
            slope = jnp.broadcast_to(decay[block, pl.ds(point, 1), :], (STEP, LANES))
            amp_l = jnp.broadcast_to(lor_amp[block, pl.ds(point, 1), :], (STEP, LANES))
            amp_g = jnp.broadcast_to(gau_amp[block, pl.ds(point, 1), :], (STEP, LANES))
            pieces = []
            for piece in range(WINDOW // STEP):
                sq = square[piece * STEP : (piece + 1) * STEP, here]
                power = sq * slope
                value = amp_l / (1.0 - power) + amp_g * jnp.exp2(power)
                pieces.append(value.astype(jnp.bfloat16))
            blank = jnp.zeros((STEP, LANES), jnp.bfloat16)
            for stage in range(STAGES):
                hop = 1 << stage
                on = bits[block, stage] > 0
                shifted = [blank] * hop + pieces
                stay = pieces + [blank] * hop
                pieces = [jnp.where(on, a, b) for a, b in zip(shifted, stay)]
            profiles.append(jnp.concatenate(pieces, axis=0))
            weight = table[block, pl.ds(pl.multiple_of(point * rows, rows), rows), :]
            packed = jnp.concatenate([weight, weight], axis=0).astype(jnp.bfloat16)
            weights.append(
                jnp.concatenate(
                    [
                        packed * route[block, part * 2 * rows : (part + 1) * 2 * rows, :]
                        for part in range(nwave)
                    ],
                    axis=0,
                )
            )
        accum[:, 0:SPAN] = lax.dot_general(
            jnp.concatenate(weights, axis=1),
            jnp.concatenate(profiles, axis=1),
            (((1,), (1,)), ((), ())),
            preferred_element_type=jnp.float32,
        )
        even_a = pltpu.roll(accum[0:total_rows, 0:LANES], QUARTER, 1)
        even_b = pltpu.roll(accum[0:total_rows, LANES : 2 * LANES], QUARTER, 1)
        odd_a = accum[total_rows : 2 * total_rows, 0:LANES]
        odd_b = accum[total_rows : 2 * total_rows, LANES : 2 * LANES]
        edge[rows : rows + total_rows, :] = jnp.where(low_lane, odd_b, even_a)
        above = edge[rows - mixes : rows - mixes + total_rows, :]
        below = edge[rows + mixes : rows + mixes + total_rows, :]
        joined = (odd_a + jnp.where(low_lane, even_a, even_b)) + jnp.where(low_lane, above, below)
        for tile in range(nwave):
            send[phase, tile, inner] = joined[tile * rows : (tile + 1) * rows]

    def plane_copy(phase, step):
        other = lax.rem(me_w + step, nwave)
        return pltpu.make_async_remote_copy(
            src_ref=send.at[phase, other],
            dst_ref=recv.at[phase, me_w],
            send_sem=send_sem.at[phase, other],
            recv_sem=recv_sem.at[phase, me_w],
            device_id=(me_s, other),
            device_id_type=MESH,
        )

    def plane_total(phase):
        total = send[phase, me_w]
        for step in range(1, nwave):
            other = lax.rem(me_w + step, nwave)
            pltpu.make_async_remote_copy(
                src_ref=send.at[phase, other],
                dst_ref=recv.at[phase, other],
                send_sem=send_sem.at[phase, other],
                recv_sem=recv_sem.at[phase, other],
                device_id=(me_s, other),
                device_id_type=MESH,
            ).wait_recv()
            total = total + recv[phase, other]
        return total

    def axis_copy(phase):
        group = group_of(phase)
        return pltpu.make_async_remote_copy(
            src_ref=zsend.at[phase],
            dst_ref=zrecv.at[me_s],
            send_sem=zsend_sem.at[phase],
            recv_sem=zrecv_sem.at[me_s],
            device_id=(group, me_w),
            device_id_type=MESH,
        )

    def advance(step, carry):
        phase = lax.div(step, chunk)
        inner = lax.rem(step, chunk)
        evaluate(phase, inner)

        @pl.when(step == chunk)
        def _():
            pl.semaphore_wait(barrier, nwave + nspecies - 2)

        @pl.when(jnp.logical_and(inner == 0, phase > 0))
        def _():
            for other in range(1, nwave):
                plane_copy(phase - 1, other).start()

        @pl.when(jnp.logical_and(inner == chunk - 1, phase > 0))
        def _():
            zsend[phase - 1] = plane_total(phase - 1)
            axis_copy(phase - 1).start()

        return carry

    lax.fori_loop(0, points, advance, 0)
    for step in range(1, nwave):
        plane_copy(last, step).start()
    total = plane_total(last)
    for step in range(1, nspecies):
        other = lax.rem(me_s + step, nspecies)
        pltpu.make_async_remote_copy(
            src_ref=zsend.at[0],
            dst_ref=zrecv.at[other],
            send_sem=zsend_sem.at[0],
            recv_sem=zrecv_sem.at[other],
            device_id=(other, me_w),
            device_id_type=MESH,
        ).wait_recv()
        total = total + zrecv[other]
    for mix in range(mixes):
        for half in range(2):
            out[mix, :, half * LANES : (half + 1) * LANES] = total[:, half * mixes + mix, :]
    for phase in range(nspecies):
        for step in range(1, nwave):
            plane_copy(phase, step).wait_send()
        if phase < last:
            axis_copy(phase).wait_send()


def per_device(
    dest_tiles,
    line_counts,
    wing_widths,
    species_ids,
    offsets,
    strengths,
    doppler,
    lorentz,
    energy,
    temp_scale,
    press_scale,
    inverse_temp,
    abundances,
):
    nspecies = lax.axis_size("species")
    nwave = lax.axis_size("wave")
    nblocks = dest_tiles.shape[1]
    mixes, _, sub, points = abundances.shape
    chunk = points // nspecies
    rows = 2 * mixes
    total_rows = nwave * rows
    lines = nblocks * LANES
    sizes = (nspecies, nwave, nblocks, points, mixes, sub)
    smem = pl.BlockSpec(memory_space=pltpu.SMEM)
    vmem = pl.BlockSpec(memory_space=pltpu.VMEM)
    table = pltpu.VMEM((nblocks, points, LANES), jnp.float32)
    return pl.pallas_call(
        functools.partial(kernel, sizes),
        out_shape=jax.ShapeDtypeStruct((mixes, chunk, 2 * LANES), jnp.float32),
        in_specs=[smem] * 7 + [vmem] * 6,
        out_specs=vmem,
        scratch_shapes=[
            pltpu.VMEM((WINDOW, lines), jnp.float32),
            table,
            table,
            table,
            pltpu.VMEM((nblocks, points * rows, LANES), jnp.float32),
            pltpu.VMEM((nblocks, STAGES, STEP, LANES), jnp.float32),
            pltpu.VMEM((nblocks, 2 * total_rows, LANES), jnp.bfloat16),
            pltpu.VMEM((mixes, sub, points, LANES), jnp.float32),
            pltpu.VMEM((2 * total_rows, 2 * LANES), jnp.float32),
            pltpu.VMEM((total_rows + 2 * rows, LANES), jnp.float32),
            pltpu.VMEM((nspecies, nwave, chunk, rows, LANES), jnp.float32),
            pltpu.VMEM((nspecies, nwave, chunk, rows, LANES), jnp.float32),
            pltpu.VMEM((nspecies, chunk, rows, LANES), jnp.float32),
            pltpu.VMEM((nspecies, chunk, rows, LANES), jnp.float32),
            pltpu.SemaphoreType.DMA((nspecies, nwave)),
            pltpu.SemaphoreType.DMA((nspecies, nwave)),
            pltpu.SemaphoreType.DMA((nspecies,)),
            pltpu.SemaphoreType.DMA((nspecies,)),
        ],
        compiler_params=pltpu.CompilerParams(collective_id=0, has_side_effects=True),
    )(
        dest_tiles.reshape(1, nblocks),
        line_counts,
        wing_widths,
        temp_scale,
        press_scale,
        inverse_temp,
        abundances,
        species_ids,
        offsets,
        strengths,
        doppler,
        lorentz,
        energy,
    )


def solution(mesh):
    lines = P("species", "wave")
    return jax.shard_map(
        per_device,
        mesh=mesh,
        in_specs=(P("species", "wave", None),)
        + (lines,) * 8
        + (P(), P(), P(), P(None, "species", None, None)),
        out_specs=P(None, "species", "wave"),
        check_vma=False,
    )
```

```python
import functools

import jax
import jax.numpy as jnp
from jax import lax
from jax.experimental import pallas as pl
from jax.experimental.pallas import tpu as pltpu
from jax.sharding import PartitionSpec as P

LANES = 128
HALO = 64
STEP = 16
WINDOW = LANES + STEP
QUARTER = 64
SPAN = QUARTER + 2 * HALO
STAGES = 2
FAR = 1e37
RATIO = False
PAIR = 2
MESH = pl.DeviceIdType.MESH


def column(ref, count):
    rows = lax.broadcasted_iota(jnp.int32, (count, LANES), 0)
    out = jnp.zeros((count, LANES), jnp.float32)
    for index in range(count):
        out = jnp.where(rows == index, ref[index], out)
    return out


def kernel(
    sizes,
    tiles,
    counts,
    wings,
    temp,
    press,
    inverse,
    abund,
    kinds,
    offsets,
    strengths,
    doppler,
    lorentz,
    energy,
    out,
    square,
    decay,
    lor_amp,
    gau_amp,
    table,
    bits,
    route,
    coef,
    accum,
    edge,
    send,
    recv,
    zsend,
    zrecv,
    send_sem,
    recv_sem,
    zsend_sem,
    zrecv_sem,
):
    nspecies, nwave, nblocks, points, mixes, sub = sizes
    chunk = points // nspecies
    turns = chunk // PAIR
    last = nspecies - 1
    rows = 2 * mixes
    tile_rows = 2 * rows
    total_rows = nwave * rows
    me_s = lax.axis_index("species")
    me_w = lax.axis_index("wave")

    barrier = pltpu.get_barrier_semaphore()
    for step in range(1, nwave):
        pl.semaphore_signal(
            barrier,
            inc=1,
            device_id=(me_s, lax.rem(me_w + step, nwave)),
            device_id_type=MESH,
        )
    for step in range(1, nspecies):
        pl.semaphore_signal(
            barrier,
            inc=1,
            device_id=(lax.rem(me_s + step, nspecies), me_w),
            device_id_type=MESH,
        )

    temp_col = column(temp, points)
    press_col = column(press, points)
    inverse_col = column(inverse, points)
    lane_row = lax.broadcasted_iota(jnp.int32, (1, LANES), 1)
    local = lax.broadcasted_iota(jnp.int32, (WINDOW, LANES), 0).astype(jnp.float32) - HALO
    row_point = lax.broadcasted_iota(jnp.int32, (points, LANES), 0)
    row16 = lax.broadcasted_iota(jnp.int32, (2 * rows, LANES), 0)
    row_quarter = (
        lax.rem(lax.div(row16, mixes), 2) * 2 + lax.div(row16, rows)
    ).astype(jnp.float32)
    for mix in range(mixes):
        for kind in range(sub):
            value = jnp.zeros((points, LANES), jnp.float32)
            for point in range(points):
                value = jnp.where(row_point == point, abund[mix, 0, kind, point], value)
            coef[mix, kind] = value

    def prepare(block, carry):
        here = pl.ds(pl.multiple_of(block * LANES, LANES), LANES)
        center = offsets[:, here]
        quarter = jnp.clip(jnp.floor(center * (1.0 / QUARTER)), 0.0, 3.0)
        center = center - quarter * float(QUARTER)
        hop = jnp.clip(jnp.floor(center * (1.0 / STEP)), 0.0, float(QUARTER // STEP - 1))
        reach = wings[0, block].astype(jnp.float32)
        offset = (local + hop * float(STEP)) - center
        sq = offset * offset
        square[:, here] = jnp.where(sq <= reach * reach, sq, FAR)
        hop_int = hop.astype(jnp.int32)
        for stage in range(STAGES):
            bit = (hop_int >> stage) & 1
            bits[block, stage] = jnp.broadcast_to(bit.astype(jnp.float32), (STEP, LANES))
        gauss = 2.35482 * (temp_col * doppler[:, here])
        lor = 2.0 * (press_col * lorentz[:, here])
        g2 = gauss * gauss
        g4 = g2 * g2
        l2 = lor * lor
        l4 = l2 * l2
        poly = (
            g4 * gauss
            + 2.69269 * g4 * lor
            + 2.42843 * (g2 * gauss) * l2
            + 4.47163 * g2 * (l2 * lor)
            + 0.07842 * gauss * l4
            + l4 * lor
        )
        width = jnp.exp(0.2 * jnp.log(poly))
        inv = 1.0 / width
        ratio = lor * inv
        eta = ratio * (1.36603 + ratio * (-0.47719 + ratio * 0.11116))
        decay[block] = -4.0 * (inv * inv)
        amp_l = eta * inv * (4.0 * 0.15915494)
        amp_g = (1.0 - eta) * inv * 0.9394373
        if RATIO:
            gau_amp[block] = amp_g / amp_l
        else:
            lor_amp[block] = amp_l
            gau_amp[block] = amp_g
        boltz = jnp.exp(-(inverse_col * energy[:, here]))
        strength = jnp.where(lane_row < counts[0, block], strengths[:, here], 0.0)
        kind_row = kinds[:, here]
        for mix in range(mixes):
            mixed = coef[mix, 0]
            for kind in range(1, sub):
                mixed = jnp.where(kind_row == kind, coef[mix, kind], mixed)
            mixed = (mixed * strength) * boltz
            if RATIO:
                mixed = mixed * amp_l
            for half in range(2):
                table[block, pl.ds(half * mixes + mix, points, stride=rows), :] = mixed
        chosen = jnp.where(row_quarter == quarter, 1.0, 0.0)
        target = tiles[0, block]
        for tile in range(nwave):
            route[block, tile * tile_rows : (tile + 1) * tile_rows, :] = jnp.where(
                target == tile, chosen, 0.0
            ).astype(jnp.bfloat16)
        return carry

    lax.fori_loop(0, nblocks, prepare, 0, unroll=4)

    accum[...] = jnp.zeros(accum.shape, jnp.float32)
    edge[...] = jnp.zeros(edge.shape, jnp.float32)
    low_lane = lax.broadcasted_iota(jnp.int32, (total_rows, LANES), 1) < QUARTER
    lane_all = lax.broadcasted_iota(jnp.int32, (LANES, 2 * total_rows), 1)
    odd_lane = lax.rem(lax.div(lane_all, rows), 2) == 1

    def group_of(phase):
        if nspecies % 2:
            return lax.rem(me_s + 1 + phase, nspecies)
        pairs = nspecies // 2
        ahead = pairs - 1 - lax.div(phase, 2)
        other = lax.rem(me_s + 1 + lax.rem(phase, 2), 2)
        return lax.rem(lax.div(me_s, 2) + ahead, pairs) * 2 + other

    def evaluate(step):
        base = group_of(lax.div(step, turns)) * chunk + lax.rem(step, turns) * PAIR
        spots = range(PAIR)
        weights = [[] for _ in spots]
        profiles = [[] for _ in spots]

        def one(slot, block):
            point = base + slot
            here = pl.ds(block * LANES, LANES)
            slope = jnp.broadcast_to(decay[block, pl.ds(point, 1), :], (STEP, LANES))
            amp_g = jnp.broadcast_to(gau_amp[block, pl.ds(point, 1), :], (STEP, LANES))
            if not RATIO:
                amp_l = jnp.broadcast_to(lor_amp[block, pl.ds(point, 1), :], (STEP, LANES))
            pieces = []
            for piece in range(WINDOW // STEP):
                sq = square[piece * STEP : (piece + 1) * STEP, here]
                power = sq * slope
                if RATIO:
                    value = 1.0 / (1.0 - power) + amp_g * jnp.exp2(power)
                else:
                    value = amp_l / (1.0 - power) + amp_g * jnp.exp2(power)
                pieces.append(value.astype(jnp.bfloat16))
            blank = jnp.zeros((STEP, LANES), jnp.bfloat16)
            for stage in range(STAGES):
                hop = 1 << stage
                on = bits[block, stage] > 0
                shifted = [blank] * hop + pieces
                stay = pieces + [blank] * hop
                pieces = [jnp.where(on, a, b) for a, b in zip(shifted, stay)]
            profiles[slot].append(jnp.concatenate(pieces, axis=0))
            weight = table[block, pl.ds(pl.multiple_of(point * rows, rows), rows), :]
            packed = jnp.concatenate([weight, weight], axis=0).astype(jnp.bfloat16)
            weights[slot].append(
                jnp.concatenate(
                    [
                        packed * route[block, tile * tile_rows : (tile + 1) * tile_rows, :]
                        for tile in range(nwave)
                    ],
                    axis=0,
                )
            )

        for slot in spots:
            for block in range(nblocks):
                one(slot, block)
            accum[slot] = lax.dot_general(
                jnp.concatenate(profiles[slot], axis=1),
                jnp.concatenate(weights[slot], axis=1),
                (((1,), (1,)), ((), ())),
                preferred_element_type=jnp.float32,
            )

    def finish(step):
        phase = lax.div(step, turns)
        first = lax.rem(step, turns) * PAIR
        for slot in range(PAIR):
            near = jnp.where(odd_lane, accum[slot, 0:LANES, :], accum[slot, QUARTER:SPAN, :]).T
            far = jnp.concatenate([accum[slot, LANES:SPAN, :], accum[slot, 0:QUARTER, :]], axis=0).T

            def part(array, parity):
                return jnp.concatenate(
                    [
                        array[(2 * tile + parity) * rows : (2 * tile + parity + 1) * rows]
                        for tile in range(nwave)
                    ],
                    axis=0,
                )

            edge[slot, rows : rows + total_rows, :] = jnp.where(low_lane, part(far, 1), part(far, 0))
            above = edge[slot, rows - mixes : rows - mixes + total_rows, :]
            below = edge[slot, rows + mixes : rows + mixes + total_rows, :]
            joined = (part(near, 0) + part(near, 1)) + jnp.where(low_lane, above, below)
            for tile in range(nwave):
                send[phase, tile, first + slot] = joined[tile * rows : (tile + 1) * rows]

    def plane_copy(phase, step, sent=None):
        other = lax.rem(me_w + step, nwave)
        index = phase if sent is None else last + sent
        part = pl.ds(0, chunk) if sent is None else pl.ds(sent * PAIR, PAIR)
        return pltpu.make_async_remote_copy(
            src_ref=send.at[phase, other, part],
            dst_ref=recv.at[phase, me_w, part],
            send_sem=send_sem.at[index, other],
            recv_sem=recv_sem.at[index, me_w],
            device_id=(me_s, other),
            device_id_type=MESH,
        )

    def plane_total(phase, sent=None):
        index = phase if sent is None else last + sent
        part = pl.ds(0, chunk) if sent is None else pl.ds(sent * PAIR, PAIR)
        total = send[phase, me_w, part]
        for step in range(1, nwave):
            other = lax.rem(me_w + step, nwave)
            pltpu.make_async_remote_copy(
                src_ref=send.at[phase, other, part],
                dst_ref=recv.at[phase, other, part],
                send_sem=send_sem.at[index, other],
                recv_sem=recv_sem.at[index, other],
                device_id=(me_s, other),
                device_id_type=MESH,
            ).wait_recv()
            total = total + recv[phase, other, part]
        return total

    def axis_copy(phase):
        group = group_of(phase)
        return pltpu.make_async_remote_copy(
            src_ref=zsend.at[phase],
            dst_ref=zrecv.at[me_s],
            send_sem=zsend_sem.at[phase],
            recv_sem=zrecv_sem.at[me_s],
            device_id=(group, me_w),
            device_id_type=MESH,
        )

    def relay(phase):
        zsend[phase] = plane_total(phase)
        axis_copy(phase).start()

    def advance(step, carry):
        finish(jnp.maximum(step - 1, 0))
        evaluate(step)
        phase = lax.div(step, turns)
        turn = lax.rem(step, turns)

        @pl.when(step == turns)
        def _():
            pl.semaphore_wait(barrier, nwave + nspecies - 2)

        @pl.when(jnp.logical_and(turn == 0, phase > 0))
        def _():
            for other in range(1, nwave):
                plane_copy(phase - 1, other).start()

        @pl.when(jnp.logical_and(turn == 0, phase > 1))
        def _():
            relay(phase - 2)

        for sent in range(turns - 1):

            @pl.when(step == last * turns + sent + 1)
            def _():
                for other in range(1, nwave):
                    plane_copy(last, other, sent).start()

        return carry

    lax.fori_loop(0, nspecies * turns, advance, 0)
    finish(nspecies * turns - 1)
    for step in range(1, nwave):
        plane_copy(last, step, turns - 1).start()
    relay(last - 1)
    parts = [plane_total(last, sent) for sent in range(turns)]
    total = parts[0] if turns == 1 else jnp.concatenate(parts, axis=0)
    for step in range(1, nspecies):
        other = lax.rem(me_s + step, nspecies)
        pltpu.make_async_remote_copy(
            src_ref=zsend.at[0],
            dst_ref=zrecv.at[other],
            send_sem=zsend_sem.at[0],
            recv_sem=zrecv_sem.at[other],
            device_id=(other, me_w),
            device_id_type=MESH,
        ).wait_recv()
        total = total + zrecv[other]
    for mix in range(mixes):
        for half in range(2):
            out[mix, :, half * LANES : (half + 1) * LANES] = total[:, half * mixes + mix, :]
    for step in range(1, nwave):
        for phase in range(last):
            plane_copy(phase, step).wait_send()
        for sent in range(turns):
            plane_copy(last, step, sent).wait_send()
    for phase in range(last):
        axis_copy(phase).wait_send()


def per_device(
    dest_tiles,
    line_counts,
    wing_widths,
    species_ids,
    offsets,
    strengths,
    doppler,
    lorentz,
    energy,
    temp_scale,
    press_scale,
    inverse_temp,
    abundances,
):
    nspecies = lax.axis_size("species")
    nwave = lax.axis_size("wave")
    nblocks = dest_tiles.shape[1]
    mixes, _, sub, points = abundances.shape
    chunk = points // nspecies
    turns = chunk // PAIR
    last = nspecies - 1
    rows = 2 * mixes
    total_rows = nwave * rows
    lines = nblocks * LANES
    sizes = (nspecies, nwave, nblocks, points, mixes, sub)
    smem = pl.BlockSpec(memory_space=pltpu.SMEM)
    vmem = pl.BlockSpec(memory_space=pltpu.VMEM)
    table = pltpu.VMEM((nblocks, points, LANES), jnp.float32)
    return pl.pallas_call(
        functools.partial(kernel, sizes),
        out_shape=jax.ShapeDtypeStruct((mixes, chunk, 2 * LANES), jnp.float32),
        in_specs=[smem] * 7 + [vmem] * 6,
        out_specs=vmem,
        scratch_shapes=[
            pltpu.VMEM((WINDOW, lines), jnp.float32),
            table,
            table,
            table,
            pltpu.VMEM((nblocks, points * rows, LANES), jnp.float32),
            pltpu.VMEM((nblocks, STAGES, STEP, LANES), jnp.float32),
            pltpu.VMEM((nblocks, 2 * total_rows, LANES), jnp.bfloat16),
            pltpu.VMEM((mixes, sub, points, LANES), jnp.float32),
            pltpu.VMEM((PAIR, SPAN, 2 * total_rows), jnp.float32),
            pltpu.VMEM((PAIR, total_rows + 2 * rows, LANES), jnp.float32),
            pltpu.VMEM((nspecies, nwave, chunk, rows, LANES), jnp.float32),
            pltpu.VMEM((nspecies, nwave, chunk, rows, LANES), jnp.float32),
            pltpu.VMEM((nspecies, chunk, rows, LANES), jnp.float32),
            pltpu.VMEM((nspecies, chunk, rows, LANES), jnp.float32),
            pltpu.SemaphoreType.DMA((last + turns, nwave)),
            pltpu.SemaphoreType.DMA((last + turns, nwave)),
            pltpu.SemaphoreType.DMA((nspecies,)),
            pltpu.SemaphoreType.DMA((nspecies,)),
        ],
        compiler_params=pltpu.CompilerParams(collective_id=0, has_side_effects=True),
    )(
        dest_tiles.reshape(1, nblocks),
        line_counts,
        wing_widths,
        temp_scale,
        press_scale,
        inverse_temp,
        abundances,
        species_ids,
        offsets,
        strengths,
        doppler,
        lorentz,
        energy,
    )


def solution(mesh):
    lines = P("species", "wave")
    return jax.shard_map(
        per_device,
        mesh=mesh,
        in_specs=(P("species", "wave", None),)
        + (lines,) * 8
        + (P(), P(), P(), P(None, "species", None, None)),
        out_specs=P(None, "species", "wave"),
        check_vma=False,
    )
```

```python
import functools

import jax
import jax.numpy as jnp
from jax import lax
from jax.experimental import pallas as pl
from jax.experimental.pallas import tpu as pltpu
from jax.sharding import PartitionSpec as P

LANES = 128
HALO = 64
STEP = 16
WINDOW = LANES + STEP
QUARTER = 64
SPAN = QUARTER + 2 * HALO
STAGES = 2
FAR = 1e37
RATIO = False
PAIR = 2
MESH = pl.DeviceIdType.MESH


def column(ref, count):
    rows = lax.broadcasted_iota(jnp.int32, (count, LANES), 0)
    out = jnp.zeros((count, LANES), jnp.float32)
    for index in range(count):
        out = jnp.where(rows == index, ref[index], out)
    return out


def kernel(
    sizes,
    *refs,
):
    nspecies, nwave, nblocks, points, mixes, sub = sizes
    sources, out, scratch = refs[:13], refs[13], refs[14:]
    inputs, input_sem = scratch[:13], scratch[13]
    (
        tiles,
        counts,
        wings,
        temp,
        press,
        inverse,
        abund,
        kinds,
        offsets,
        strengths,
        doppler,
        lorentz,
        energy,
    ) = inputs
    (
        square,
        decay,
        lor_amp,
        gau_amp,
        table,
        bits,
        route,
        coef,
        accum,
        edge,
        send,
        recv,
        zsend,
        zrecv,
        send_sem,
        recv_sem,
        zsend_sem,
        zrecv_sem,
    ) = scratch[14:]
    chunk = points // nspecies
    turns = chunk // PAIR
    last = nspecies - 1
    rows = 2 * mixes
    tile_rows = 2 * rows
    total_rows = nwave * rows
    me_s = lax.axis_index("species")
    me_w = lax.axis_index("wave")

    loads = [
        pltpu.make_async_copy(source, target, input_sem.at[index])
        for index, (source, target) in enumerate(zip(sources, inputs))
    ]
    for load in loads:
        load.start()
    barrier = pltpu.get_barrier_semaphore()
    for step in range(1, nwave):
        pl.semaphore_signal(
            barrier,
            inc=1,
            device_id=(me_s, lax.rem(me_w + step, nwave)),
            device_id_type=MESH,
        )
    for step in range(1, nspecies):
        pl.semaphore_signal(
            barrier,
            inc=1,
            device_id=(lax.rem(me_s + step, nspecies), me_w),
            device_id_type=MESH,
        )

    for load in loads:
        load.wait()
    temp_col = column(temp, points)
    press_col = column(press, points)
    inverse_col = column(inverse, points)
    lane_row = lax.broadcasted_iota(jnp.int32, (1, LANES), 1)
    local = lax.broadcasted_iota(jnp.int32, (WINDOW, LANES), 0).astype(jnp.float32) - HALO
    row_point = lax.broadcasted_iota(jnp.int32, (points, LANES), 0)
    row16 = lax.broadcasted_iota(jnp.int32, (2 * rows, LANES), 0)
    row_quarter = (
        lax.rem(lax.div(row16, mixes), 2) * 2 + lax.div(row16, rows)
    ).astype(jnp.float32)
    for mix in range(mixes):
        for kind in range(sub):
            value = jnp.zeros((points, LANES), jnp.float32)
            for point in range(points):
                value = jnp.where(row_point == point, abund[mix, 0, kind, point], value)
            coef[mix, kind] = value

    def prepare(block, carry):
        here = pl.ds(pl.multiple_of(block * LANES, LANES), LANES)
        center = offsets[:, here]
        quarter = jnp.clip(jnp.floor(center * (1.0 / QUARTER)), 0.0, 3.0)
        center = center - quarter * float(QUARTER)
        hop = jnp.clip(jnp.floor(center * (1.0 / STEP)), 0.0, float(QUARTER // STEP - 1))
        reach = wings[0, block].astype(jnp.float32)
        offset = (local + hop * float(STEP)) - center
        sq = offset * offset
        square[:, here] = jnp.where(sq <= reach * reach, sq, FAR)
        hop_int = hop.astype(jnp.int32)
        for stage in range(STAGES):
            bit = (hop_int >> stage) & 1
            bits[block, stage] = jnp.broadcast_to(bit.astype(jnp.float32), (STEP, LANES))
        gauss = 2.35482 * (temp_col * doppler[:, here])
        lor = 2.0 * (press_col * lorentz[:, here])
        g2 = gauss * gauss
        g4 = g2 * g2
        l2 = lor * lor
        l4 = l2 * l2
        poly = (
            g4 * gauss
            + 2.69269 * g4 * lor
            + 2.42843 * (g2 * gauss) * l2
            + 4.47163 * g2 * (l2 * lor)
            + 0.07842 * gauss * l4
            + l4 * lor
        )
        width = jnp.exp(0.2 * jnp.log(poly))
        inv = 1.0 / width
        ratio = lor * inv
        eta = ratio * (1.36603 + ratio * (-0.47719 + ratio * 0.11116))
        decay[block] = -4.0 * (inv * inv)
        amp_l = eta * inv * (4.0 * 0.15915494)
        amp_g = (1.0 - eta) * inv * 0.9394373
        if RATIO:
            gau_amp[block] = amp_g / amp_l
        else:
            lor_amp[block] = amp_l
            gau_amp[block] = amp_g
        boltz = jnp.exp(-(inverse_col * energy[:, here]))
        strength = jnp.where(lane_row < counts[0, block], strengths[:, here], 0.0)
        kind_row = kinds[:, here]
        for mix in range(mixes):
            mixed = coef[mix, 0]
            for kind in range(1, sub):
                mixed = jnp.where(kind_row == kind, coef[mix, kind], mixed)
            mixed = (mixed * strength) * boltz
            if RATIO:
                mixed = mixed * amp_l
            for half in range(2):
                table[block, pl.ds(half * mixes + mix, points, stride=rows), :] = mixed
        chosen = jnp.where(row_quarter == quarter, 1.0, 0.0)
        target = tiles[0, block]
        for tile in range(nwave):
            route[block, tile * tile_rows : (tile + 1) * tile_rows, :] = jnp.where(
                target == tile, chosen, 0.0
            ).astype(jnp.bfloat16)
        return carry

    lax.fori_loop(0, nblocks, prepare, 0, unroll=4)

    accum[...] = jnp.zeros(accum.shape, jnp.float32)
    edge[...] = jnp.zeros(edge.shape, jnp.float32)
    low_lane = lax.broadcasted_iota(jnp.int32, (total_rows, LANES), 1) < QUARTER
    lane_all = lax.broadcasted_iota(jnp.int32, (LANES, 2 * total_rows), 1)
    odd_lane = lax.rem(lax.div(lane_all, rows), 2) == 1

    def group_of(phase):
        if nspecies % 2:
            return lax.rem(me_s + 1 + phase, nspecies)
        pairs = nspecies // 2
        ahead = pairs - 1 - lax.div(phase, 2)
        other = lax.rem(me_s + 1 + lax.rem(phase, 2), 2)
        return lax.rem(lax.div(me_s, 2) + ahead, pairs) * 2 + other

    def evaluate(step):
        base = group_of(lax.div(step, turns)) * chunk + lax.rem(step, turns) * PAIR
        spots = range(PAIR)
        weights = [[] for _ in spots]
        profiles = [[] for _ in spots]

        def one(slot, block):
            point = base + slot
            here = pl.ds(block * LANES, LANES)
            slope = jnp.broadcast_to(decay[block, pl.ds(point, 1), :], (STEP, LANES))
            amp_g = jnp.broadcast_to(gau_amp[block, pl.ds(point, 1), :], (STEP, LANES))
            if not RATIO:
                amp_l = jnp.broadcast_to(lor_amp[block, pl.ds(point, 1), :], (STEP, LANES))
            pieces = []
            for piece in range(WINDOW // STEP):
                sq = square[piece * STEP : (piece + 1) * STEP, here]
                power = sq * slope
                if RATIO:
                    value = 1.0 / (1.0 - power) + amp_g * jnp.exp2(power)
                else:
                    value = amp_l / (1.0 - power) + amp_g * jnp.exp2(power)
                pieces.append(value.astype(jnp.bfloat16))
            blank = jnp.zeros((STEP, LANES), jnp.bfloat16)
            for stage in range(STAGES):
                hop = 1 << stage
                on = bits[block, stage] > 0
                shifted = [blank] * hop + pieces
                stay = pieces + [blank] * hop
                pieces = [jnp.where(on, a, b) for a, b in zip(shifted, stay)]
            profiles[slot].append(jnp.concatenate(pieces, axis=0))
            weight = table[block, pl.ds(pl.multiple_of(point * rows, rows), rows), :]
            packed = jnp.concatenate([weight, weight], axis=0).astype(jnp.bfloat16)
            weights[slot].append(
                jnp.concatenate(
                    [
                        packed * route[block, tile * tile_rows : (tile + 1) * tile_rows, :]
                        for tile in range(nwave)
                    ],
                    axis=0,
                )
            )

        for slot in spots:
            for block in range(nblocks):
                one(slot, block)
            accum[slot] = lax.dot_general(
                jnp.concatenate(profiles[slot], axis=1),
                jnp.concatenate(weights[slot], axis=1),
                (((1,), (1,)), ((), ())),
                preferred_element_type=jnp.float32,
            )

    def finish(step, phase):
        first = lax.rem(step, turns) * PAIR
        for slot in range(PAIR):
            near = jnp.where(odd_lane, accum[slot, 0:LANES, :], accum[slot, QUARTER:SPAN, :]).T
            far = jnp.concatenate([accum[slot, LANES:SPAN, :], accum[slot, 0:QUARTER, :]], axis=0).T

            def part(array, parity):
                return jnp.concatenate(
                    [
                        array[(2 * tile + parity) * rows : (2 * tile + parity + 1) * rows]
                        for tile in range(nwave)
                    ],
                    axis=0,
                )

            edge[slot, rows : rows + total_rows, :] = jnp.where(low_lane, part(far, 1), part(far, 0))
            above = edge[slot, rows - mixes : rows - mixes + total_rows, :]
            below = edge[slot, rows + mixes : rows + mixes + total_rows, :]
            joined = (part(near, 0) + part(near, 1)) + jnp.where(low_lane, above, below)
            for tile in range(nwave):
                send[phase, tile, first + slot] = joined[tile * rows : (tile + 1) * rows]

    def plane_copy(phase, step, sent=None):
        other = lax.rem(me_w + step, nwave)
        index = phase if sent is None else last + sent
        part = pl.ds(0, chunk) if sent is None else pl.ds(sent * PAIR, PAIR)
        return pltpu.make_async_remote_copy(
            src_ref=send.at[phase, other, part],
            dst_ref=recv.at[phase, me_w, part],
            send_sem=send_sem.at[index, other],
            recv_sem=recv_sem.at[index, me_w],
            device_id=(me_s, other),
            device_id_type=MESH,
        )

    def plane_total(phase, sent=None):
        index = phase if sent is None else last + sent
        part = pl.ds(0, chunk) if sent is None else pl.ds(sent * PAIR, PAIR)
        total = send[phase, me_w, part]
        for step in range(1, nwave):
            other = lax.rem(me_w + step, nwave)
            pltpu.make_async_remote_copy(
                src_ref=send.at[phase, other, part],
                dst_ref=recv.at[phase, other, part],
                send_sem=send_sem.at[index, other],
                recv_sem=recv_sem.at[index, other],
                device_id=(me_s, other),
                device_id_type=MESH,
            ).wait_recv()
            total = total + recv[phase, other, part]
        return total

    def axis_copy(phase):
        group = group_of(phase)
        return pltpu.make_async_remote_copy(
            src_ref=zsend.at[phase],
            dst_ref=zrecv.at[me_s],
            send_sem=zsend_sem.at[phase],
            recv_sem=zrecv_sem.at[me_s],
            device_id=(group, me_w),
            device_id_type=MESH,
        )

    def relay(phase):
        zsend[phase] = plane_total(phase)
        axis_copy(phase).start()

    def advance(step, carry):
        before = jnp.maximum(step - 1, 0)
        finish(before, jnp.where(step == last * turns, nspecies, lax.div(before, turns)))
        evaluate(step)
        phase = lax.div(step, turns)
        turn = lax.rem(step, turns)

        @pl.when(step == turns)
        def _():
            pl.semaphore_wait(barrier, nwave + nspecies - 2)

        @pl.when(jnp.logical_and(turn == 0, jnp.logical_and(phase > 0, phase < last)))
        def _():
            for other in range(1, nwave):
                plane_copy(phase - 1, other).start()

        @pl.when(step == last * turns - 1)
        def _():
            finish(step, last - 1)
            for other in range(1, nwave):
                plane_copy(last - 1, other).start()

        @pl.when(jnp.logical_and(turn == 0, phase > 1))
        def _():
            relay(phase - 2)

        for sent in range(turns - 1):

            @pl.when(step == last * turns + sent + 1)
            def _():
                for other in range(1, nwave):
                    plane_copy(last, other, sent).start()

        return carry

    lax.fori_loop(0, nspecies * turns, advance, 0)
    finish(nspecies * turns - 1, last)
    for step in range(1, nwave):
        plane_copy(last, step, turns - 1).start()
    relay(last - 1)
    parts = [plane_total(last, sent) for sent in range(turns)]
    total = parts[0] if turns == 1 else jnp.concatenate(parts, axis=0)
    for step in range(1, nspecies):
        other = lax.rem(me_s + step, nspecies)
        pltpu.make_async_remote_copy(
            src_ref=zsend.at[0],
            dst_ref=zrecv.at[other],
            send_sem=zsend_sem.at[0],
            recv_sem=zrecv_sem.at[other],
            device_id=(other, me_w),
            device_id_type=MESH,
        ).wait_recv()
        total = total + zrecv[other]
    for mix in range(mixes):
        for half in range(2):
            out[mix, :, half * LANES : (half + 1) * LANES] = total[:, half * mixes + mix, :]
    for step in range(1, nwave):
        for phase in range(last):
            plane_copy(phase, step).wait_send()
        for sent in range(turns):
            plane_copy(last, step, sent).wait_send()
    for phase in range(last):
        axis_copy(phase).wait_send()


def per_device(
    dest_tiles,
    line_counts,
    wing_widths,
    species_ids,
    offsets,
    strengths,
    doppler,
    lorentz,
    energy,
    temp_scale,
    press_scale,
    inverse_temp,
    abundances,
):
    nspecies = lax.axis_size("species")
    nwave = lax.axis_size("wave")
    nblocks = dest_tiles.shape[1]
    mixes, _, sub, points = abundances.shape
    chunk = points // nspecies
    turns = chunk // PAIR
    last = nspecies - 1
    rows = 2 * mixes
    total_rows = nwave * rows
    lines = nblocks * LANES
    sizes = (nspecies, nwave, nblocks, points, mixes, sub)
    operands = (
        dest_tiles.reshape(1, nblocks),
        line_counts,
        wing_widths,
        temp_scale,
        press_scale,
        inverse_temp,
        abundances,
        species_ids,
        offsets,
        strengths,
        doppler,
        lorentz,
        energy,
    )
    operands = tuple(pltpu.with_memory_space_constraint(array, pltpu.HBM) for array in operands)
    spaces = [pltpu.SMEM] * 7 + [pltpu.VMEM] * 6
    table = pltpu.VMEM((nblocks, points, LANES), jnp.float32)
    return pl.pallas_call(
        functools.partial(kernel, sizes),
        out_shape=jax.ShapeDtypeStruct((mixes, chunk, 2 * LANES), jnp.float32),
        in_specs=[pl.BlockSpec(memory_space=pltpu.HBM)] * len(operands),
        out_specs=pl.BlockSpec(memory_space=pltpu.VMEM),
        scratch_shapes=[space(array.shape, array.dtype) for space, array in zip(spaces, operands)]
        + [
            pltpu.SemaphoreType.DMA((len(operands),)),
            pltpu.VMEM((WINDOW, lines), jnp.float32),
            table,
            table,
            table,
            pltpu.VMEM((nblocks, points * rows, LANES), jnp.float32),
            pltpu.VMEM((nblocks, STAGES, STEP, LANES), jnp.float32),
            pltpu.VMEM((nblocks, 2 * total_rows, LANES), jnp.bfloat16),
            pltpu.VMEM((mixes, sub, points, LANES), jnp.float32),
            pltpu.VMEM((PAIR, SPAN, 2 * total_rows), jnp.float32),
            pltpu.VMEM((PAIR, total_rows + 2 * rows, LANES), jnp.float32),
            pltpu.VMEM((nspecies + 1, nwave, chunk, rows, LANES), jnp.float32),
            pltpu.VMEM((nspecies, nwave, chunk, rows, LANES), jnp.float32),
            pltpu.VMEM((nspecies, chunk, rows, LANES), jnp.float32),
            pltpu.VMEM((nspecies, chunk, rows, LANES), jnp.float32),
            pltpu.SemaphoreType.DMA((last + turns, nwave)),
            pltpu.SemaphoreType.DMA((last + turns, nwave)),
            pltpu.SemaphoreType.DMA((nspecies,)),
            pltpu.SemaphoreType.DMA((nspecies,)),
        ],
        compiler_params=pltpu.CompilerParams(collective_id=0, has_side_effects=True, vmem_limit_bytes=24 << 20),
    )(*operands)


def solution(mesh):
    lines = P("species", "wave")
    return jax.shard_map(
        per_device,
        mesh=mesh,
        in_specs=(P("species", "wave", None),)
        + (lines,) * 8
        + (P(), P(), P(), P(None, "species", None, None)),
        out_specs=P(None, "species", "wave"),
        check_vma=False,
    )
```

```python
import functools

import jax
import jax.numpy as jnp
from jax import lax
from jax.experimental import pallas as pl
from jax.experimental.pallas import tpu as pltpu
from jax.sharding import PartitionSpec as P

LANES = 128
HALO = 64
STEP = 16
WINDOW = LANES + STEP
QUARTER = 64
SPAN = QUARTER + 2 * HALO
STAGES = 2
FAR = 1e37
MESH = pl.DeviceIdType.MESH


def column(ref, count):
    rows = lax.broadcasted_iota(jnp.int32, (count, LANES), 0)
    out = jnp.zeros((count, LANES), jnp.float32)
    for index in range(count):
        out = jnp.where(rows == index, ref[index], out)
    return out


def kernel(
    sizes,
    *refs,
):
    nspecies, nwave, nblocks, points, mixes, sub = sizes
    sources, out, scratch = refs[:13], refs[13], refs[14:]
    inputs, input_sem = scratch[:13], scratch[13]
    (
        tiles,
        counts,
        wings,
        temp,
        press,
        inverse,
        abund,
        kinds,
        offsets,
        strengths,
        doppler,
        lorentz,
        energy,
    ) = inputs
    (
        square,
        decay,
        lor_amp,
        gau_amp,
        table,
        bits,
        route,
        coef,
        accum,
        edge,
        send,
        recv,
        zsend,
        zrecv,
        send_sem,
        recv_sem,
        zsend_sem,
        zrecv_sem,
    ) = scratch[14:]
    chunk = points // nspecies
    last = nspecies - 1
    rows = 2 * mixes
    tile_rows = 2 * rows
    total_rows = nwave * rows
    me_s = lax.axis_index("species")
    me_w = lax.axis_index("wave")

    loads = [
        pltpu.make_async_copy(source, target, input_sem.at[index])
        for index, (source, target) in enumerate(zip(sources, inputs))
    ]
    for load in loads:
        load.start()
    barrier = pltpu.get_barrier_semaphore()
    for step in range(1, nwave):
        pl.semaphore_signal(
            barrier,
            inc=1,
            device_id=(me_s, lax.rem(me_w + step, nwave)),
            device_id_type=MESH,
        )
    for step in range(1, nspecies):
        pl.semaphore_signal(
            barrier,
            inc=1,
            device_id=(lax.rem(me_s + step, nspecies), me_w),
            device_id_type=MESH,
        )

    for load in loads:
        load.wait()
    temp_col = column(temp, points)
    press_col = column(press, points)
    inverse_col = column(inverse, points)
    lane_row = lax.broadcasted_iota(jnp.int32, (1, LANES), 1)
    local = lax.broadcasted_iota(jnp.int32, (WINDOW, LANES), 0).astype(jnp.float32) - HALO
    row_point = lax.broadcasted_iota(jnp.int32, (points, LANES), 0)
    row16 = lax.broadcasted_iota(jnp.int32, (2 * rows, LANES), 0)
    row_quarter = (
        lax.rem(lax.div(row16, mixes), 2) * 2 + lax.div(row16, rows)
    ).astype(jnp.float32)
    for mix in range(mixes):
        for kind in range(sub):
            value = jnp.zeros((points, LANES), jnp.float32)
            for point in range(points):
                value = jnp.where(row_point == point, abund[mix, 0, kind, point], value)
            coef[mix, kind] = value

    def prepare(block, carry):
        here = pl.ds(pl.multiple_of(block * LANES, LANES), LANES)
        center = offsets[:, here]
        quarter = jnp.clip(jnp.floor(center * (1.0 / QUARTER)), 0.0, 3.0)
        center = center - quarter * float(QUARTER)
        hop = jnp.clip(jnp.floor(center * (1.0 / STEP)), 0.0, float(QUARTER // STEP - 1))
        reach = wings[0, block].astype(jnp.float32)
        offset = local - (center - hop * float(STEP))
        sq = offset * offset
        square[:, here] = jnp.where(sq <= reach * reach, sq, FAR)
        hop_int = hop.astype(jnp.int32)
        for stage in range(STAGES):
            bit = (hop_int >> stage) & 1
            bits[block, stage] = jnp.broadcast_to(bit.astype(jnp.float32), (STEP, LANES))
        gauss = 2.35482 * (temp_col * doppler[:, here])
        lor = 2.0 * (press_col * lorentz[:, here])
        g2 = gauss * gauss
        g4 = g2 * g2
        l2 = lor * lor
        l4 = l2 * l2
        poly = (
            g4 * gauss
            + 2.69269 * g4 * lor
            + 2.42843 * (g2 * gauss) * l2
            + 4.47163 * g2 * (l2 * lor)
            + 0.07842 * gauss * l4
            + l4 * lor
        )
        width = jnp.exp(0.2 * jnp.log(poly))
        inv = 1.0 / width
        ratio = lor * inv
        eta = ratio * (1.36603 + ratio * (-0.47719 + ratio * 0.11116))
        decay[block] = -4.0 * (inv * inv)
        amp_l = eta * inv * (4.0 * 0.15915494)
        amp_g = (1.0 - eta) * inv * 0.9394373
        lor_amp[block] = amp_l
        gau_amp[block] = amp_g
        boltz = jnp.exp(-(inverse_col * energy[:, here]))
        strength = jnp.where(lane_row < counts[0, block], strengths[:, here], 0.0)
        kind_row = kinds[:, here]
        for mix in range(mixes):
            mixed = coef[mix, 0]
            for kind in range(1, sub):
                mixed = jnp.where(kind_row == kind, coef[mix, kind], mixed)
            mixed = (mixed * strength) * boltz
            for half in range(2):
                table[block, pl.ds(half * mixes + mix, points, stride=rows), :] = mixed
        chosen = jnp.where(row_quarter == quarter, 1.0, 0.0).astype(jnp.bfloat16)
        blank16 = jnp.zeros_like(chosen)
        target = tiles[0, block]
        for tile in range(nwave):
            route[block, tile * tile_rows : (tile + 1) * tile_rows, :] = jnp.where(
                target == tile, chosen, blank16
            )
        return carry

    lax.fori_loop(0, nblocks, prepare, 0, unroll=4)

    accum[...] = jnp.zeros(accum.shape, jnp.float32)
    edge[...] = jnp.zeros(edge.shape, jnp.float32)
    low_lane = lax.broadcasted_iota(jnp.int32, (total_rows, LANES), 1) < QUARTER
    lane_all = lax.broadcasted_iota(jnp.int32, (LANES, 2 * total_rows), 1)
    odd_lane = lax.rem(lax.div(lane_all, rows), 2) == 1

    def group_of(phase):
        if nspecies % 2:
            return lax.rem(me_s + 1 + phase, nspecies)
        pairs = nspecies // 2
        ahead = pairs - 1 - lax.div(phase, 2)
        other = lax.rem(me_s + 1 + lax.rem(phase, 2), 2)
        return lax.rem(lax.div(me_s, 2) + ahead, pairs) * 2 + other

    def evaluate(phase):
        base = group_of(phase) * chunk
        spots = range(chunk)
        weights = [[] for _ in spots]
        profiles = [[] for _ in spots]

        def one(slot, block):
            point = base + slot
            here = pl.ds(block * LANES, LANES)
            slope = jnp.broadcast_to(decay[block, pl.ds(point, 1), :], (STEP, LANES))
            amp_g = jnp.broadcast_to(gau_amp[block, pl.ds(point, 1), :], (STEP, LANES))
            amp_l = jnp.broadcast_to(lor_amp[block, pl.ds(point, 1), :], (STEP, LANES))
            pieces = []
            for piece in range(WINDOW // STEP):
                sq = square[piece * STEP : (piece + 1) * STEP, here]
                power = sq * slope
                value = amp_l / (1.0 - power) + amp_g * jnp.exp2(power)
                pieces.append(value.astype(jnp.bfloat16))
            blank = jnp.zeros((STEP, LANES), jnp.bfloat16)
            for stage in range(STAGES):
                hop = 1 << stage
                on = bits[block, stage] > 0
                shifted = [blank] * hop + pieces
                stay = pieces + [blank] * hop
                pieces = [jnp.where(on, a, b) for a, b in zip(shifted, stay)]
            profiles[slot].append(jnp.concatenate(pieces, axis=0))
            weight = table[block, pl.ds(pl.multiple_of(point * rows, rows), rows), :]
            packed = jnp.concatenate([weight, weight], axis=0).astype(jnp.bfloat16)
            weights[slot].append(
                jnp.concatenate(
                    [
                        packed * route[block, tile * tile_rows : (tile + 1) * tile_rows, :]
                        for tile in range(nwave)
                    ],
                    axis=0,
                )
            )

        for slot in spots:
            for block in range(nblocks):
                one(slot, block)
            accum[slot] = lax.dot_general(
                jnp.concatenate(profiles[slot], axis=1),
                jnp.concatenate(weights[slot], axis=1),
                (((1,), (1,)), ((), ())),
                preferred_element_type=jnp.float32,
            )

    def finish(phase):
        for slot in range(chunk):
            near = jnp.where(odd_lane, accum[slot, 0:LANES, :], accum[slot, QUARTER:SPAN, :]).T
            far = jnp.concatenate([accum[slot, LANES:SPAN, :], accum[slot, 0:QUARTER, :]], axis=0).T

            def part(array, parity):
                return jnp.concatenate(
                    [
                        array[(2 * tile + parity) * rows : (2 * tile + parity + 1) * rows]
                        for tile in range(nwave)
                    ],
                    axis=0,
                )

            edge[slot, rows : rows + total_rows, :] = jnp.where(low_lane, part(far, 1), part(far, 0))
            above = edge[slot, rows - mixes : rows - mixes + total_rows, :]
            below = edge[slot, rows + mixes : rows + mixes + total_rows, :]
            joined = (part(near, 0) + part(near, 1)) + jnp.where(low_lane, above, below)
            for tile in range(nwave):
                send[phase, tile, slot] = joined[tile * rows : (tile + 1) * rows]

    def plane_copy(phase, step):
        other = lax.rem(me_w + step, nwave)
        return pltpu.make_async_remote_copy(
            src_ref=send.at[phase, other],
            dst_ref=recv.at[phase, me_w],
            send_sem=send_sem.at[phase, other],
            recv_sem=recv_sem.at[phase, me_w],
            device_id=(me_s, other),
            device_id_type=MESH,
        )

    def plane_total(phase):
        total = send[phase, me_w]
        for step in range(1, nwave):
            other = lax.rem(me_w + step, nwave)
            pltpu.make_async_remote_copy(
                src_ref=send.at[phase, other],
                dst_ref=recv.at[phase, other],
                send_sem=send_sem.at[phase, other],
                recv_sem=recv_sem.at[phase, other],
                device_id=(me_s, other),
                device_id_type=MESH,
            ).wait_recv()
            total = total + recv[phase, other]
        return total

    def axis_copy(phase):
        group = group_of(phase)
        return pltpu.make_async_remote_copy(
            src_ref=zsend.at[phase],
            dst_ref=zrecv.at[me_s],
            send_sem=zsend_sem.at[phase],
            recv_sem=zrecv_sem.at[me_s],
            device_id=(group, me_w),
            device_id_type=MESH,
        )

    def relay(phase):
        zsend[phase] = plane_total(phase)
        axis_copy(phase).start()

    def spread(phase):
        for step in range(1, nwave):
            plane_copy(phase, step).start()

    def advance(phase, carry):
        ready = jnp.logical_and(phase > 0, phase < last)
        finish(jnp.where(ready, phase - 1, nspecies))
        evaluate(phase)

        @pl.when(phase == 1)
        def _():
            pl.semaphore_wait(barrier, nwave + nspecies - 2)

        @pl.when(ready)
        def _():
            spread(phase - 1)

        @pl.when(phase == last - 1)
        def _():
            finish(phase)
            spread(phase)

        @pl.when(jnp.logical_and(phase > 1, phase < last))
        def _():
            relay(phase - 2)

        return carry

    lax.fori_loop(0, nspecies, advance, 0)
    finish(last)
    spread(last)
    relay(last - 2)
    relay(last - 1)
    total = plane_total(last)
    for step in range(1, nspecies):
        other = lax.rem(me_s + step, nspecies)
        pltpu.make_async_remote_copy(
            src_ref=zsend.at[0],
            dst_ref=zrecv.at[other],
            send_sem=zsend_sem.at[0],
            recv_sem=zrecv_sem.at[other],
            device_id=(other, me_w),
            device_id_type=MESH,
        ).wait_recv()
        total = total + zrecv[other]
    for mix in range(mixes):
        for half in range(2):
            out[mix, :, half * LANES : (half + 1) * LANES] = total[:, half * mixes + mix, :]
    for phase in range(nspecies):
        for step in range(1, nwave):
            plane_copy(phase, step).wait_send()
    for phase in range(last):
        axis_copy(phase).wait_send()


def per_device(
    dest_tiles,
    line_counts,
    wing_widths,
    species_ids,
    offsets,
    strengths,
    doppler,
    lorentz,
    energy,
    temp_scale,
    press_scale,
    inverse_temp,
    abundances,
):
    nspecies = lax.axis_size("species")
    nwave = lax.axis_size("wave")
    nblocks = dest_tiles.shape[1]
    mixes, _, sub, points = abundances.shape
    chunk = points // nspecies
    rows = 2 * mixes
    total_rows = nwave * rows
    lines = nblocks * LANES
    sizes = (nspecies, nwave, nblocks, points, mixes, sub)
    operands = (
        dest_tiles.reshape(1, nblocks),
        line_counts,
        wing_widths,
        temp_scale,
        press_scale,
        inverse_temp,
        abundances,
        species_ids,
        offsets,
        strengths,
        doppler,
        lorentz,
        energy,
    )
    operands = tuple(pltpu.with_memory_space_constraint(array, pltpu.HBM) for array in operands)
    spaces = [pltpu.SMEM] * 7 + [pltpu.VMEM] * 6
    table = pltpu.VMEM((nblocks, points, LANES), jnp.float32)
    return pl.pallas_call(
        functools.partial(kernel, sizes),
        out_shape=jax.ShapeDtypeStruct((mixes, chunk, 2 * LANES), jnp.float32),
        in_specs=[pl.BlockSpec(memory_space=pltpu.HBM)] * len(operands),
        out_specs=pl.BlockSpec(memory_space=pltpu.VMEM),
        scratch_shapes=[space(array.shape, array.dtype) for space, array in zip(spaces, operands)]
        + [
            pltpu.SemaphoreType.DMA((len(operands),)),
            pltpu.VMEM((WINDOW, lines), jnp.float32),
            table,
            table,
            table,
            pltpu.VMEM((nblocks, points * rows, LANES), jnp.float32),
            pltpu.VMEM((nblocks, STAGES, STEP, LANES), jnp.float32),
            pltpu.VMEM((nblocks, 2 * total_rows, LANES), jnp.bfloat16),
            pltpu.VMEM((mixes, sub, points, LANES), jnp.float32),
            pltpu.VMEM((chunk, SPAN, 2 * total_rows), jnp.float32),
            pltpu.VMEM((chunk, total_rows + 2 * rows, LANES), jnp.float32),
            pltpu.VMEM((nspecies + 1, nwave, chunk, rows, LANES), jnp.float32),
            pltpu.VMEM((nspecies, nwave, chunk, rows, LANES), jnp.float32),
            pltpu.VMEM((nspecies, chunk, rows, LANES), jnp.float32),
            pltpu.VMEM((nspecies, chunk, rows, LANES), jnp.float32),
            pltpu.SemaphoreType.DMA((nspecies, nwave)),
            pltpu.SemaphoreType.DMA((nspecies, nwave)),
            pltpu.SemaphoreType.DMA((nspecies,)),
            pltpu.SemaphoreType.DMA((nspecies,)),
        ],
        compiler_params=pltpu.CompilerParams(collective_id=0, has_side_effects=True, vmem_limit_bytes=24 << 20),
    )(*operands)


def solution(mesh):
    lines = P("species", "wave")
    return jax.shard_map(
        per_device,
        mesh=mesh,
        in_specs=(P("species", "wave", None),)
        + (lines,) * 8
        + (P(), P(), P(), P(None, "species", None, None)),
        out_specs=P(None, "species", "wave"),
        check_vma=False,
    )
```

```python
import functools

import jax
import jax.numpy as jnp
from jax import lax
from jax.experimental import pallas as pl
from jax.experimental.pallas import tpu as pltpu
from jax.sharding import PartitionSpec as P

LANES = 128
HALO = 64
STEP = 16
WINDOW = LANES + STEP
QUARTER = 64
SPAN = QUARTER + 2 * HALO
STAGES = 2
FAR = 1e37
MESH = pl.DeviceIdType.MESH


def column(ref, count):
    rows = lax.broadcasted_iota(jnp.int32, (count, LANES), 0)
    out = jnp.zeros((count, LANES), jnp.float32)
    for index in range(count):
        out = jnp.where(rows == index, ref[index], out)
    return out


def kernel(
    sizes,
    *refs,
):
    nspecies, nwave, nblocks, points, mixes, sub = sizes
    sources, out, scratch = refs[:13], refs[13], refs[14:]
    inputs, input_sem = scratch[:13], scratch[13]
    (
        tiles,
        counts,
        wings,
        temp,
        press,
        inverse,
        abund,
        kinds,
        offsets,
        strengths,
        doppler,
        lorentz,
        energy,
    ) = inputs
    (
        square,
        decay,
        gau_amp,
        table,
        bits,
        route,
        coef,
        accum,
        edge,
        send,
        recv,
        zsend,
        zrecv,
        send_sem,
        recv_sem,
        zsend_sem,
        zrecv_sem,
    ) = scratch[14:]
    chunk = points // nspecies
    last = nspecies - 1
    rows = 2 * mixes
    tile_rows = 2 * rows
    total_rows = nwave * rows
    me_s = lax.axis_index("species")
    me_w = lax.axis_index("wave")

    loads = [
        pltpu.make_async_copy(source, target, input_sem.at[index])
        for index, (source, target) in enumerate(zip(sources, inputs))
    ]
    for load in loads:
        load.start()
    barrier = pltpu.get_barrier_semaphore()
    for step in range(1, nwave):
        pl.semaphore_signal(
            barrier,
            inc=1,
            device_id=(me_s, lax.rem(me_w + step, nwave)),
            device_id_type=MESH,
        )
    for step in range(1, nspecies):
        pl.semaphore_signal(
            barrier,
            inc=1,
            device_id=(lax.rem(me_s + step, nspecies), me_w),
            device_id_type=MESH,
        )

    for load in loads:
        load.wait()
    temp_col = column(temp, points)
    press_col = column(press, points)
    inverse_col = column(inverse, points)
    lane_row = lax.broadcasted_iota(jnp.int32, (1, LANES), 1)
    local = lax.broadcasted_iota(jnp.int32, (WINDOW, LANES), 0).astype(jnp.float32) - HALO
    row_point = lax.broadcasted_iota(jnp.int32, (points, LANES), 0)
    row16 = lax.broadcasted_iota(jnp.int32, (2 * rows, LANES), 0)
    row_quarter = (
        lax.rem(lax.div(row16, mixes), 2) * 2 + lax.div(row16, rows)
    ).astype(jnp.float32)
    for mix in range(mixes):
        for kind in range(sub):
            value = jnp.zeros((points, LANES), jnp.float32)
            for point in range(points):
                value = jnp.where(row_point == point, abund[mix, 0, kind, point], value)
            coef[mix, kind] = value

    def prepare(block, carry):
        here = pl.ds(pl.multiple_of(block * LANES, LANES), LANES)
        center = offsets[:, here]
        quarter = jnp.clip(jnp.floor(center * (1.0 / QUARTER)), 0.0, 3.0)
        center = center - quarter * float(QUARTER)
        hop = jnp.clip(jnp.floor(center * (1.0 / STEP)), 0.0, float(QUARTER // STEP - 1))
        reach = wings[0, block].astype(jnp.float32)
        offset = local - (center - hop * float(STEP))
        sq = offset * offset
        square[:, here] = jnp.where(sq <= reach * reach, sq, FAR)
        hop_int = hop.astype(jnp.int32)
        for stage in range(STAGES):
            bit = (hop_int >> stage) & 1
            bits[block, stage] = jnp.broadcast_to(bit.astype(jnp.float32), (STEP, LANES))
        gauss = 2.35482 * (temp_col * doppler[:, here])
        lor = 2.0 * (press_col * lorentz[:, here])
        g2 = gauss * gauss
        g4 = g2 * g2
        l2 = lor * lor
        l4 = l2 * l2
        poly = (
            g4 * gauss
            + 2.69269 * g4 * lor
            + 2.42843 * (g2 * gauss) * l2
            + 4.47163 * g2 * (l2 * lor)
            + 0.07842 * gauss * l4
            + l4 * lor
        )
        width = jnp.exp(0.2 * jnp.log(poly))
        inv = 1.0 / width
        ratio = lor * inv
        eta = ratio * (1.36603 + ratio * (-0.47719 + ratio * 0.11116))
        decay[block] = -4.0 * (inv * inv)
        amp_l = eta * inv * (4.0 * 0.15915494)
        amp_g = (1.0 - eta) * inv * 0.9394373
        gau_amp[block] = amp_g / amp_l
        boltz = jnp.exp(-(inverse_col * energy[:, here]))
        strength = jnp.where(lane_row < counts[0, block], strengths[:, here], 0.0)
        kind_row = kinds[:, here]
        for mix in range(mixes):
            mixed = coef[mix, 0]
            for kind in range(1, sub):
                mixed = jnp.where(kind_row == kind, coef[mix, kind], mixed)
            mixed = (mixed * strength) * boltz
            mixed = mixed * amp_l
            for half in range(2):
                table[block, pl.ds(half * mixes + mix, points, stride=rows), :] = mixed
        chosen = jnp.where(row_quarter == quarter, 1.0, 0.0).astype(jnp.bfloat16)
        blank16 = jnp.zeros_like(chosen)
        target = tiles[0, block]
        for tile in range(nwave):
            route[block, tile * tile_rows : (tile + 1) * tile_rows, :] = jnp.where(
                target == tile, chosen, blank16
            )
        return carry

    lax.fori_loop(0, nblocks, prepare, 0, unroll=4)

    accum[...] = jnp.zeros(accum.shape, jnp.float32)
    edge[...] = jnp.zeros(edge.shape, jnp.float32)
    low_lane = lax.broadcasted_iota(jnp.int32, (total_rows, LANES), 1) < QUARTER
    lane_all = lax.broadcasted_iota(jnp.int32, (LANES, 2 * total_rows), 1)
    odd_lane = lax.rem(lax.div(lane_all, rows), 2) == 1

    def group_of(phase):
        if nspecies % 2:
            return lax.rem(me_s + 1 + phase, nspecies)
        pairs = nspecies // 2
        ahead = pairs - 1 - lax.div(phase, 2)
        other = lax.rem(me_s + 1 + lax.rem(phase, 2), 2)
        return lax.rem(lax.div(me_s, 2) + ahead, pairs) * 2 + other

    def evaluate(phase):
        base = group_of(phase) * chunk
        spots = range(chunk)
        weights = [[] for _ in spots]
        profiles = [[] for _ in spots]

        def one(slot, block):
            point = base + slot
            here = pl.ds(block * LANES, LANES)
            slope = jnp.broadcast_to(decay[block, pl.ds(point, 1), :], (STEP, LANES))
            amp_g = jnp.broadcast_to(gau_amp[block, pl.ds(point, 1), :], (STEP, LANES))
            pieces = []
            for piece in range(WINDOW // STEP):
                sq = square[piece * STEP : (piece + 1) * STEP, here]
                power = sq * slope
                value = 1.0 / (1.0 - power) + amp_g * jnp.exp2(power)
                pieces.append(value.astype(jnp.bfloat16))
            blank = jnp.zeros((STEP, LANES), jnp.bfloat16)
            for stage in range(STAGES):
                hop = 1 << stage
                on = bits[block, stage] > 0
                shifted = [blank] * hop + pieces
                stay = pieces + [blank] * hop
                pieces = [jnp.where(on, a, b) for a, b in zip(shifted, stay)]
            profiles[slot].append(jnp.concatenate(pieces, axis=0))
            weight = table[block, pl.ds(pl.multiple_of(point * rows, rows), rows), :]
            packed = jnp.concatenate([weight, weight], axis=0).astype(jnp.bfloat16)
            weights[slot].append(
                jnp.concatenate(
                    [
                        packed * route[block, tile * tile_rows : (tile + 1) * tile_rows, :]
                        for tile in range(nwave)
                    ],
                    axis=0,
                )
            )

        for slot in spots:
            for block in range(nblocks):
                one(slot, block)
            accum[slot] = lax.dot_general(
                jnp.concatenate(profiles[slot], axis=1),
                jnp.concatenate(weights[slot], axis=1),
                (((1,), (1,)), ((), ())),
                preferred_element_type=jnp.float32,
            )

    def finish(phase):
        for slot in range(chunk):
            near = jnp.where(odd_lane, accum[slot, 0:LANES, :], accum[slot, QUARTER:SPAN, :]).T
            far = jnp.concatenate([accum[slot, LANES:SPAN, :], accum[slot, 0:QUARTER, :]], axis=0).T

            def part(array, parity):
                return jnp.concatenate(
                    [
                        array[(2 * tile + parity) * rows : (2 * tile + parity + 1) * rows]
                        for tile in range(nwave)
                    ],
                    axis=0,
                )

            edge[slot, rows : rows + total_rows, :] = jnp.where(low_lane, part(far, 1), part(far, 0))
            above = edge[slot, rows - mixes : rows - mixes + total_rows, :]
            below = edge[slot, rows + mixes : rows + mixes + total_rows, :]
            joined = (part(near, 0) + part(near, 1)) + jnp.where(low_lane, above, below)
            for tile in range(nwave):
                send[phase, tile, slot] = joined[tile * rows : (tile + 1) * rows]

    def plane_copy(phase, step):
        other = lax.rem(me_w + step, nwave)
        return pltpu.make_async_remote_copy(
            src_ref=send.at[phase, other],
            dst_ref=recv.at[phase, me_w],
            send_sem=send_sem.at[phase, other],
            recv_sem=recv_sem.at[phase, me_w],
            device_id=(me_s, other),
            device_id_type=MESH,
        )

    def plane_total(phase):
        total = send[phase, me_w]
        for step in range(1, nwave):
            other = lax.rem(me_w + step, nwave)
            pltpu.make_async_remote_copy(
                src_ref=send.at[phase, other],
                dst_ref=recv.at[phase, other],
                send_sem=send_sem.at[phase, other],
                recv_sem=recv_sem.at[phase, other],
                device_id=(me_s, other),
                device_id_type=MESH,
            ).wait_recv()
            total = total + recv[phase, other]
        return total

    def axis_copy(phase):
        group = group_of(phase)
        return pltpu.make_async_remote_copy(
            src_ref=zsend.at[phase],
            dst_ref=zrecv.at[me_s],
            send_sem=zsend_sem.at[phase],
            recv_sem=zrecv_sem.at[me_s],
            device_id=(group, me_w),
            device_id_type=MESH,
        )

    def relay(phase):
        zsend[phase] = plane_total(phase)
        axis_copy(phase).start()

    def spread(phase):
        for step in range(1, nwave):
            plane_copy(phase, step).start()

    def advance(phase, carry):
        ready = jnp.logical_and(phase > 0, phase < last)
        finish(jnp.where(ready, phase - 1, nspecies))
        evaluate(phase)

        @pl.when(phase == 1)
        def _():
            pl.semaphore_wait(barrier, nwave + nspecies - 2)

        @pl.when(ready)
        def _():
            spread(phase - 1)

        @pl.when(phase == last - 1)
        def _():
            finish(phase)
            spread(phase)

        @pl.when(jnp.logical_and(phase > 1, phase < last))
        def _():
            relay(phase - 2)

        return carry

    lax.fori_loop(0, nspecies, advance, 0)
    finish(last)
    spread(last)
    relay(last - 2)
    relay(last - 1)
    total = plane_total(last)
    for step in range(1, nspecies):
        other = lax.rem(me_s + step, nspecies)
        pltpu.make_async_remote_copy(
            src_ref=zsend.at[0],
            dst_ref=zrecv.at[other],
            send_sem=zsend_sem.at[0],
            recv_sem=zrecv_sem.at[other],
            device_id=(other, me_w),
            device_id_type=MESH,
        ).wait_recv()
        total = total + zrecv[other]
    for mix in range(mixes):
        for half in range(2):
            out[mix, :, half * LANES : (half + 1) * LANES] = total[:, half * mixes + mix, :]
    for phase in range(nspecies):
        for step in range(1, nwave):
            plane_copy(phase, step).wait_send()
    for phase in range(last):
        axis_copy(phase).wait_send()


def per_device(
    dest_tiles,
    line_counts,
    wing_widths,
    species_ids,
    offsets,
    strengths,
    doppler,
    lorentz,
    energy,
    temp_scale,
    press_scale,
    inverse_temp,
    abundances,
):
    nspecies = lax.axis_size("species")
    nwave = lax.axis_size("wave")
    nblocks = dest_tiles.shape[1]
    mixes, _, sub, points = abundances.shape
    chunk = points // nspecies
    rows = 2 * mixes
    total_rows = nwave * rows
    lines = nblocks * LANES
    sizes = (nspecies, nwave, nblocks, points, mixes, sub)
    operands = (
        dest_tiles.reshape(1, nblocks),
        line_counts,
        wing_widths,
        temp_scale,
        press_scale,
        inverse_temp,
        abundances,
        species_ids,
        offsets,
        strengths,
        doppler,
        lorentz,
        energy,
    )
    operands = tuple(pltpu.with_memory_space_constraint(array, pltpu.HBM) for array in operands)
    spaces = [pltpu.SMEM] * 7 + [pltpu.VMEM] * 6
    table = pltpu.VMEM((nblocks, points, LANES), jnp.float32)
    return pl.pallas_call(
        functools.partial(kernel, sizes),
        out_shape=jax.ShapeDtypeStruct((mixes, chunk, 2 * LANES), jnp.float32),
        in_specs=[pl.BlockSpec(memory_space=pltpu.HBM)] * len(operands),
        out_specs=pl.BlockSpec(memory_space=pltpu.VMEM),
        scratch_shapes=[space(array.shape, array.dtype) for space, array in zip(spaces, operands)]
        + [
            pltpu.SemaphoreType.DMA((len(operands),)),
            pltpu.VMEM((WINDOW, lines), jnp.float32),
            table,
            table,
            pltpu.VMEM((nblocks, points * rows, LANES), jnp.float32),
            pltpu.VMEM((nblocks, STAGES, STEP, LANES), jnp.float32),
            pltpu.VMEM((nblocks, 2 * total_rows, LANES), jnp.bfloat16),
            pltpu.VMEM((mixes, sub, points, LANES), jnp.float32),
            pltpu.VMEM((chunk, SPAN, 2 * total_rows), jnp.float32),
            pltpu.VMEM((chunk, total_rows + 2 * rows, LANES), jnp.float32),
            pltpu.VMEM((nspecies + 1, nwave, chunk, rows, LANES), jnp.float32),
            pltpu.VMEM((nspecies, nwave, chunk, rows, LANES), jnp.float32),
            pltpu.VMEM((nspecies, chunk, rows, LANES), jnp.float32),
            pltpu.VMEM((nspecies, chunk, rows, LANES), jnp.float32),
            pltpu.SemaphoreType.DMA((nspecies, nwave)),
            pltpu.SemaphoreType.DMA((nspecies, nwave)),
            pltpu.SemaphoreType.DMA((nspecies,)),
            pltpu.SemaphoreType.DMA((nspecies,)),
        ],
        compiler_params=pltpu.CompilerParams(collective_id=0, has_side_effects=True, vmem_limit_bytes=24 << 20),
    )(*operands)


def solution(mesh):
    lines = P("species", "wave")
    return jax.shard_map(
        per_device,
        mesh=mesh,
        in_specs=(P("species", "wave", None),)
        + (lines,) * 8
        + (P(), P(), P(), P(None, "species", None, None)),
        out_specs=P(None, "species", "wave"),
        check_vma=False,
    )
```

```python
import functools

import jax
import jax.numpy as jnp
from jax import lax
from jax.experimental import pallas as pl
from jax.experimental.pallas import tpu as pltpu
from jax.sharding import PartitionSpec as P

LANES = 128
HALO = 64
STEP = 16
WINDOW = LANES + STEP
QUARTER = 64
SPAN = QUARTER + 2 * HALO
STAGES = 2
FAR = 1e37
MESH = pl.DeviceIdType.MESH


def column(ref, count):
    rows = lax.broadcasted_iota(jnp.int32, (count, LANES), 0)
    out = jnp.zeros((count, LANES), jnp.float32)
    for index in range(count):
        out = jnp.where(rows == index, ref[index], out)
    return out


def kernel(
    sizes,
    *refs,
):
    nspecies, nwave, nblocks, points, mixes, sub = sizes
    sources, out, scratch = refs[:13], refs[13], refs[14:]
    inputs, input_sem = scratch[:13], scratch[13]
    (
        tiles,
        counts,
        wings,
        temp,
        press,
        inverse,
        abund,
        kinds,
        offsets,
        strengths,
        doppler,
        lorentz,
        energy,
    ) = inputs
    (
        square,
        decay,
        gau_amp,
        table,
        bits,
        route,
        coef,
        accum,
        edge,
        send,
        recv,
        zsend,
        zrecv,
        send_sem,
        recv_sem,
        zsend_sem,
        zrecv_sem,
    ) = scratch[14:]
    chunk = points // nspecies
    last = nspecies - 1
    rows = 2 * mixes
    tile_rows = 2 * rows
    total_rows = nwave * rows
    me_s = lax.axis_index("species")
    me_w = lax.axis_index("wave")

    loads = [
        pltpu.make_async_copy(source, target, input_sem.at[index])
        for index, (source, target) in enumerate(zip(sources, inputs))
    ]
    for load in loads:
        load.start()
    barrier = pltpu.get_barrier_semaphore()
    for step in range(1, nwave):
        pl.semaphore_signal(
            barrier,
            inc=1,
            device_id=(me_s, lax.rem(me_w + step, nwave)),
            device_id_type=MESH,
        )
    for step in range(1, nspecies):
        pl.semaphore_signal(
            barrier,
            inc=1,
            device_id=(lax.rem(me_s + step, nspecies), me_w),
            device_id_type=MESH,
        )

    for load in loads:
        load.wait()
    temp_col = column(temp, points)
    press_col = column(press, points)
    inverse_col = column(inverse, points)
    lane_row = lax.broadcasted_iota(jnp.int32, (1, LANES), 1)
    local = lax.broadcasted_iota(jnp.int32, (WINDOW, LANES), 0).astype(jnp.float32) - HALO
    row_point = lax.broadcasted_iota(jnp.int32, (points, LANES), 0)
    row16 = lax.broadcasted_iota(jnp.int32, (2 * rows, LANES), 0)
    row_quarter = (
        lax.rem(lax.div(row16, mixes), 2) * 2 + lax.div(row16, rows)
    ).astype(jnp.float32)
    for mix in range(mixes):
        for kind in range(sub):
            value = jnp.zeros((points, LANES), jnp.float32)
            for point in range(points):
                value = jnp.where(row_point == point, abund[mix, 0, kind, point], value)
            coef[mix, kind] = value

    def prepare(block, carry):
        here = pl.ds(pl.multiple_of(block * LANES, LANES), LANES)
        center = offsets[:, here]
        quarter = jnp.clip(jnp.floor(center * (1.0 / QUARTER)), 0.0, 3.0)
        center = center - quarter * float(QUARTER)
        hop = jnp.clip(jnp.floor(center * (1.0 / STEP)), 0.0, float(QUARTER // STEP - 1))
        reach = wings[0, block].astype(jnp.float32)
        offset = local - (center - hop * float(STEP))
        sq = offset * offset
        square[:, here] = jnp.where(sq <= reach * reach, sq, FAR)
        hop_int = hop.astype(jnp.int32)
        for stage in range(STAGES):
            bit = (hop_int >> stage) & 1
            bits[block, stage] = jnp.broadcast_to(bit.astype(jnp.float32), (STEP, LANES))
        gauss = 2.35482 * (temp_col * doppler[:, here])
        lor = 2.0 * (press_col * lorentz[:, here])
        g2 = gauss * gauss
        g4 = g2 * g2
        l2 = lor * lor
        l4 = l2 * l2
        poly = (
            g4 * gauss
            + 2.69269 * g4 * lor
            + 2.42843 * (g2 * gauss) * l2
            + 4.47163 * g2 * (l2 * lor)
            + 0.07842 * gauss * l4
            + l4 * lor
        )
        width = jnp.exp(0.2 * jnp.log(poly))
        inv = 1.0 / width
        ratio = lor * inv
        eta = ratio * (1.36603 + ratio * (-0.47719 + ratio * 0.11116))
        decay[block] = -4.0 * (inv * inv)
        amp_l = eta * inv * (4.0 * 0.15915494)
        amp_g = (1.0 - eta) * inv * 0.9394373
        gau_amp[block] = amp_g / amp_l
        boltz = jnp.exp(-(inverse_col * energy[:, here]))
        strength = jnp.where(lane_row < counts[0, block], strengths[:, here], 0.0)
        kind_row = kinds[:, here]
        for mix in range(mixes):
            mixed = coef[mix, 0]
            for kind in range(1, sub):
                mixed = jnp.where(kind_row == kind, coef[mix, kind], mixed)
            mixed = (mixed * strength) * boltz
            mixed = mixed * amp_l
            for half in range(2):
                table[block, pl.ds(half * mixes + mix, points, stride=rows), :] = mixed
        chosen = jnp.where(row_quarter == quarter, 1.0, 0.0)
        target = tiles[0, block]
        for tile in range(nwave):
            route[block, tile * tile_rows : (tile + 1) * tile_rows, :] = jnp.where(
                target == tile, chosen, 0.0
            ).astype(jnp.bfloat16)
        return carry

    lax.fori_loop(0, nblocks, prepare, 0, unroll=4)

    accum[...] = jnp.zeros(accum.shape, jnp.float32)
    edge[...] = jnp.zeros(edge.shape, jnp.float32)
    low_lane = lax.broadcasted_iota(jnp.int32, (total_rows, LANES), 1) < QUARTER
    lane_all = lax.broadcasted_iota(jnp.int32, (LANES, 2 * total_rows), 1)
    odd_lane = lax.rem(lax.div(lane_all, rows), 2) == 1

    def group_of(phase):
        if nspecies % 2:
            return lax.rem(me_s + 1 + phase, nspecies)
        pairs = nspecies // 2
        ahead = pairs - 1 - lax.div(phase, 2)
        other = lax.rem(me_s + 1 + lax.rem(phase, 2), 2)
        return lax.rem(lax.div(me_s, 2) + ahead, pairs) * 2 + other

    def evaluate(phase):
        base = group_of(phase) * chunk
        spots = range(chunk)
        weights = [[] for _ in spots]
        profiles = [[] for _ in spots]

        def one(slot, block):
            point = base + slot
            here = pl.ds(block * LANES, LANES)
            slope = jnp.broadcast_to(decay[block, pl.ds(point, 1), :], (STEP, LANES))
            amp_g = jnp.broadcast_to(gau_amp[block, pl.ds(point, 1), :], (STEP, LANES))
            pieces = []
            for piece in range(WINDOW // STEP):
                sq = square[piece * STEP : (piece + 1) * STEP, here]
                power = sq * slope
                value = 1.0 / (1.0 - power) + amp_g * jnp.exp2(power)
                pieces.append(value.astype(jnp.bfloat16))
            blank = jnp.zeros((STEP, LANES), jnp.bfloat16)
            for stage in range(STAGES):
                hop = 1 << stage
                on = bits[block, stage] > 0
                shifted = [blank] * hop + pieces
                stay = pieces + [blank] * hop
                pieces = [jnp.where(on, a, b) for a, b in zip(shifted, stay)]
            profiles[slot].append(jnp.concatenate(pieces, axis=0))
            weight = table[block, pl.ds(pl.multiple_of(point * rows, rows), rows), :]
            packed = jnp.concatenate([weight, weight], axis=0).astype(jnp.bfloat16)
            weights[slot].append(
                jnp.concatenate(
                    [
                        packed * route[block, tile * tile_rows : (tile + 1) * tile_rows, :]
                        for tile in range(nwave)
                    ],
                    axis=0,
                )
            )

        for slot in spots:
            for block in range(nblocks):
                one(slot, block)
            accum[slot] = lax.dot_general(
                jnp.concatenate(profiles[slot], axis=1),
                jnp.concatenate(weights[slot], axis=1),
                (((1,), (1,)), ((), ())),
                preferred_element_type=jnp.float32,
            )

    def finish(phase):
        for slot in range(chunk):
            near = jnp.where(odd_lane, accum[slot, 0:LANES, :], accum[slot, QUARTER:SPAN, :]).T
            far = jnp.concatenate([accum[slot, LANES:SPAN, :], accum[slot, 0:QUARTER, :]], axis=0).T

            def part(array, parity):
                return jnp.concatenate(
                    [
                        array[(2 * tile + parity) * rows : (2 * tile + parity + 1) * rows]
                        for tile in range(nwave)
                    ],
                    axis=0,
                )

            edge[slot, rows : rows + total_rows, :] = jnp.where(low_lane, part(far, 1), part(far, 0))
            above = edge[slot, rows - mixes : rows - mixes + total_rows, :]
            below = edge[slot, rows + mixes : rows + mixes + total_rows, :]
            joined = (part(near, 0) + part(near, 1)) + jnp.where(low_lane, above, below)
            for tile in range(nwave):
                send[phase, tile, slot] = joined[tile * rows : (tile + 1) * rows]

    def plane_copy(phase, step):
        other = lax.rem(me_w + step, nwave)
        return pltpu.make_async_remote_copy(
            src_ref=send.at[phase, other],
            dst_ref=recv.at[phase, me_w],
            send_sem=send_sem.at[phase, other],
            recv_sem=recv_sem.at[phase, me_w],
            device_id=(me_s, other),
            device_id_type=MESH,
        )

    def plane_total(phase):
        total = send[phase, me_w]
        for step in range(1, nwave):
            other = lax.rem(me_w + step, nwave)
            pltpu.make_async_remote_copy(
                src_ref=send.at[phase, other],
                dst_ref=recv.at[phase, other],
                send_sem=send_sem.at[phase, other],
                recv_sem=recv_sem.at[phase, other],
                device_id=(me_s, other),
                device_id_type=MESH,
            ).wait_recv()
            total = total + recv[phase, other]
        return total

    def axis_copy(phase):
        group = group_of(phase)
        return pltpu.make_async_remote_copy(
            src_ref=zsend.at[phase],
            dst_ref=zrecv.at[me_s],
            send_sem=zsend_sem.at[phase],
            recv_sem=zrecv_sem.at[me_s],
            device_id=(group, me_w),
            device_id_type=MESH,
        )

    def relay(phase):
        zsend[phase] = plane_total(phase)
        axis_copy(phase).start()

    def spread(phase):
        for step in range(1, nwave):
            plane_copy(phase, step).start()

    def advance(phase, carry):
        evaluate(phase)
        finish(phase)

        @pl.when(phase == 0)
        def _():
            pl.semaphore_wait(barrier, nwave + nspecies - 2)

        spread(phase)

        @pl.when(phase > 0)
        def _():
            relay(phase - 1)

        return carry

    lax.fori_loop(0, nspecies, advance, 0)
    total = plane_total(last)
    for step in range(1, nspecies):
        other = lax.rem(me_s + step, nspecies)
        pltpu.make_async_remote_copy(
            src_ref=zsend.at[0],
            dst_ref=zrecv.at[other],
            send_sem=zsend_sem.at[0],
            recv_sem=zrecv_sem.at[other],
            device_id=(other, me_w),
            device_id_type=MESH,
        ).wait_recv()
        total = total + zrecv[other]
    for mix in range(mixes):
        for half in range(2):
            out[mix, :, half * LANES : (half + 1) * LANES] = total[:, half * mixes + mix, :]
    for phase in range(nspecies):
        for step in range(1, nwave):
            plane_copy(phase, step).wait_send()
    for phase in range(last):
        axis_copy(phase).wait_send()


def per_device(
    dest_tiles,
    line_counts,
    wing_widths,
    species_ids,
    offsets,
    strengths,
    doppler,
    lorentz,
    energy,
    temp_scale,
    press_scale,
    inverse_temp,
    abundances,
):
    nspecies = lax.axis_size("species")
    nwave = lax.axis_size("wave")
    nblocks = dest_tiles.shape[1]
    mixes, _, sub, points = abundances.shape
    chunk = points // nspecies
    rows = 2 * mixes
    total_rows = nwave * rows
    lines = nblocks * LANES
    sizes = (nspecies, nwave, nblocks, points, mixes, sub)
    operands = (
        dest_tiles.reshape(1, nblocks),
        line_counts,
        wing_widths,
        temp_scale,
        press_scale,
        inverse_temp,
        abundances,
        species_ids,
        offsets,
        strengths,
        doppler,
        lorentz,
        energy,
    )
    operands = tuple(pltpu.with_memory_space_constraint(array, pltpu.HBM) for array in operands)
    spaces = [pltpu.SMEM] * 7 + [pltpu.VMEM] * 6
    table = pltpu.VMEM((nblocks, points, LANES), jnp.float32)
    return pl.pallas_call(
        functools.partial(kernel, sizes),
        out_shape=jax.ShapeDtypeStruct((mixes, chunk, 2 * LANES), jnp.float32),
        in_specs=[pl.BlockSpec(memory_space=pltpu.HBM)] * len(operands),
        out_specs=pl.BlockSpec(memory_space=pltpu.VMEM),
        scratch_shapes=[space(array.shape, array.dtype) for space, array in zip(spaces, operands)]
        + [
            pltpu.SemaphoreType.DMA((len(operands),)),
            pltpu.VMEM((WINDOW, lines), jnp.float32),
            table,
            table,
            pltpu.VMEM((nblocks, points * rows, LANES), jnp.float32),
            pltpu.VMEM((nblocks, STAGES, STEP, LANES), jnp.float32),
            pltpu.VMEM((nblocks, 2 * total_rows, LANES), jnp.bfloat16),
            pltpu.VMEM((mixes, sub, points, LANES), jnp.float32),
            pltpu.VMEM((chunk, SPAN, 2 * total_rows), jnp.float32),
            pltpu.VMEM((chunk, total_rows + 2 * rows, LANES), jnp.float32),
            pltpu.VMEM((nspecies, nwave, chunk, rows, LANES), jnp.float32),
            pltpu.VMEM((nspecies, nwave, chunk, rows, LANES), jnp.float32),
            pltpu.VMEM((nspecies, chunk, rows, LANES), jnp.float32),
            pltpu.VMEM((nspecies, chunk, rows, LANES), jnp.float32),
            pltpu.SemaphoreType.DMA((nspecies, nwave)),
            pltpu.SemaphoreType.DMA((nspecies, nwave)),
            pltpu.SemaphoreType.DMA((nspecies,)),
            pltpu.SemaphoreType.DMA((nspecies,)),
        ],
        compiler_params=pltpu.CompilerParams(collective_id=0, has_side_effects=True, vmem_limit_bytes=24 << 20),
    )(*operands)


def solution(mesh):
    lines = P("species", "wave")
    return jax.shard_map(
        per_device,
        mesh=mesh,
        in_specs=(P("species", "wave", None),)
        + (lines,) * 8
        + (P(), P(), P(), P(None, "species", None, None)),
        out_specs=P(None, "species", "wave"),
        check_vma=False,
    )
```

```python
import functools

import jax
import jax.numpy as jnp
from jax import lax
from jax.experimental import pallas as pl
from jax.experimental.pallas import tpu as pltpu
from jax.sharding import PartitionSpec as P

LANES = 128
HALO = 64
STEP = 16
WINDOW = LANES + STEP
QUARTER = 64
SPAN = QUARTER + 2 * HALO
STAGES = 2
FAR = 1e37
MESH = pl.DeviceIdType.MESH


def column(ref, count):
    rows = lax.broadcasted_iota(jnp.int32, (count, LANES), 0)
    out = jnp.zeros((count, LANES), jnp.float32)
    for index in range(count):
        out = jnp.where(rows == index, ref[index], out)
    return out


def kernel(
    sizes,
    *refs,
):
    nspecies, nwave, nblocks, points, mixes, sub = sizes
    sources, out, scratch = refs[:13], refs[13], refs[14:]
    inputs, input_sem = scratch[:13], scratch[13]
    (
        tiles,
        counts,
        wings,
        temp,
        press,
        inverse,
        abund,
        kinds,
        offsets,
        strengths,
        doppler,
        lorentz,
        energy,
    ) = inputs
    (
        square,
        decay,
        lor_amp,
        gau_amp,
        table,
        bits,
        route,
        coef,
        accum,
        edge,
        send,
        recv,
        zsend,
        zrecv,
        send_sem,
        recv_sem,
        zsend_sem,
        zrecv_sem,
    ) = scratch[14:]
    chunk = points // nspecies
    last = nspecies - 1
    rows = 2 * mixes
    tile_rows = 2 * rows
    total_rows = nwave * rows
    me_s = lax.axis_index("species")
    me_w = lax.axis_index("wave")

    loads = [
        pltpu.make_async_copy(source, target, input_sem.at[index])
        for index, (source, target) in enumerate(zip(sources, inputs))
    ]
    for load in loads:
        load.start()
    barrier = pltpu.get_barrier_semaphore()
    for step in range(1, nwave):
        pl.semaphore_signal(
            barrier,
            inc=1,
            device_id=(me_s, lax.rem(me_w + step, nwave)),
            device_id_type=MESH,
        )
    for step in range(1, nspecies):
        pl.semaphore_signal(
            barrier,
            inc=1,
            device_id=(lax.rem(me_s + step, nspecies), me_w),
            device_id_type=MESH,
        )

    for load in loads:
        load.wait()
    temp_col = column(temp, points)
    press_col = column(press, points)
    inverse_col = column(inverse, points)
    lane_row = lax.broadcasted_iota(jnp.int32, (1, LANES), 1)
    local = lax.broadcasted_iota(jnp.int32, (WINDOW, LANES), 0).astype(jnp.float32) - HALO
    row_point = lax.broadcasted_iota(jnp.int32, (points, LANES), 0)
    row16 = lax.broadcasted_iota(jnp.int32, (2 * rows, LANES), 0)
    row_quarter = (
        lax.rem(lax.div(row16, mixes), 2) * 2 + lax.div(row16, rows)
    ).astype(jnp.float32)
    for mix in range(mixes):
        for kind in range(sub):
            value = jnp.zeros((points, LANES), jnp.float32)
            for point in range(points):
                value = jnp.where(row_point == point, abund[mix, 0, kind, point], value)
            coef[mix, kind] = value

    def prepare(block, carry):
        here = pl.ds(pl.multiple_of(block * LANES, LANES), LANES)
        center = offsets[:, here]
        quarter = jnp.clip(jnp.floor(center * (1.0 / QUARTER)), 0.0, 3.0)
        center = center - quarter * float(QUARTER)
        hop = jnp.clip(jnp.floor(center * (1.0 / STEP)), 0.0, float(QUARTER // STEP - 1))
        reach = wings[0, block].astype(jnp.float32)
        offset = local - (center - hop * float(STEP))
        sq = offset * offset
        square[:, here] = jnp.where(sq <= reach * reach, sq, FAR)
        hop_int = hop.astype(jnp.int32)
        for stage in range(STAGES):
            bit = (hop_int >> stage) & 1
            bits[block, stage] = jnp.broadcast_to(bit.astype(jnp.float32), (STEP, LANES))
        gauss = 2.35482 * (temp_col * doppler[:, here])
        lor = 2.0 * (press_col * lorentz[:, here])
        g2 = gauss * gauss
        g4 = g2 * g2
        l2 = lor * lor
        l4 = l2 * l2
        poly = (
            g4 * gauss
            + 2.69269 * g4 * lor
            + 2.42843 * (g2 * gauss) * l2
            + 4.47163 * g2 * (l2 * lor)
            + 0.07842 * gauss * l4
            + l4 * lor
        )
        width = jnp.exp(0.2 * jnp.log(poly))
        inv = 1.0 / width
        ratio = lor * inv
        eta = ratio * (1.36603 + ratio * (-0.47719 + ratio * 0.11116))
        decay[block] = -4.0 * (inv * inv)
        amp_l = eta * inv * (4.0 * 0.15915494)
        amp_g = (1.0 - eta) * inv * 0.9394373
        lor_amp[block] = amp_l
        gau_amp[block] = amp_g
        boltz = jnp.exp(-(inverse_col * energy[:, here]))
        strength = jnp.where(lane_row < counts[0, block], strengths[:, here], 0.0)
        kind_row = kinds[:, here]
        for mix in range(mixes):
            mixed = coef[mix, 0]
            for kind in range(1, sub):
                mixed = jnp.where(kind_row == kind, coef[mix, kind], mixed)
            mixed = (mixed * strength) * boltz
            for half in range(2):
                table[block, pl.ds(half * mixes + mix, points, stride=rows), :] = mixed
        chosen = jnp.where(row_quarter == quarter, 1.0, 0.0)
        target = tiles[0, block]
        for tile in range(nwave):
            route[block, tile * tile_rows : (tile + 1) * tile_rows, :] = jnp.where(
                target == tile, chosen, 0.0
            ).astype(jnp.bfloat16)
        return carry

    lax.fori_loop(0, nblocks, prepare, 0, unroll=4)

    accum[...] = jnp.zeros(accum.shape, jnp.float32)
    edge[...] = jnp.zeros(edge.shape, jnp.float32)
    low_lane = lax.broadcasted_iota(jnp.int32, (total_rows, LANES), 1) < QUARTER
    lane_all = lax.broadcasted_iota(jnp.int32, (LANES, 2 * total_rows), 1)
    odd_lane = lax.rem(lax.div(lane_all, rows), 2) == 1

    def group_of(phase):
        if nspecies % 2:
            return lax.rem(me_s + 1 + phase, nspecies)
        pairs = nspecies // 2
        ahead = pairs - 1 - lax.div(phase, 2)
        other = lax.rem(me_s + 1 + lax.rem(phase, 2), 2)
        return lax.rem(lax.div(me_s, 2) + ahead, pairs) * 2 + other

    def evaluate(phase):
        base = group_of(phase) * chunk
        spots = range(chunk)
        weights = [[] for _ in spots]
        profiles = [[] for _ in spots]

        def one(slot, block):
            point = base + slot
            here = pl.ds(block * LANES, LANES)
            slope = jnp.broadcast_to(decay[block, pl.ds(point, 1), :], (STEP, LANES))
            amp_g = jnp.broadcast_to(gau_amp[block, pl.ds(point, 1), :], (STEP, LANES))
            amp_l = jnp.broadcast_to(lor_amp[block, pl.ds(point, 1), :], (STEP, LANES))
            pieces = []
            for piece in range(WINDOW // STEP):
                sq = square[piece * STEP : (piece + 1) * STEP, here]
                power = sq * slope
                value = amp_l / (1.0 - power) + amp_g * jnp.exp2(power)
                pieces.append(value.astype(jnp.bfloat16))
            blank = jnp.zeros((STEP, LANES), jnp.bfloat16)
            for stage in range(STAGES):
                hop = 1 << stage
                on = bits[block, stage] > 0
                shifted = [blank] * hop + pieces
                stay = pieces + [blank] * hop
                pieces = [jnp.where(on, a, b) for a, b in zip(shifted, stay)]
            profiles[slot].append(jnp.concatenate(pieces, axis=0))
            weight = table[block, pl.ds(pl.multiple_of(point * rows, rows), rows), :]
            packed = jnp.concatenate([weight, weight], axis=0).astype(jnp.bfloat16)
            weights[slot].append(
                jnp.concatenate(
                    [
                        packed * route[block, tile * tile_rows : (tile + 1) * tile_rows, :]
                        for tile in range(nwave)
                    ],
                    axis=0,
                )
            )

        for slot in spots:
            for block in range(nblocks):
                one(slot, block)
            accum[slot] = lax.dot_general(
                jnp.concatenate(profiles[slot], axis=1),
                jnp.concatenate(weights[slot], axis=1),
                (((1,), (1,)), ((), ())),
                preferred_element_type=jnp.float32,
            )

    def finish(phase):
        for slot in range(chunk):
            near = jnp.where(odd_lane, accum[slot, 0:LANES, :], accum[slot, QUARTER:SPAN, :]).T
            far = jnp.concatenate([accum[slot, LANES:SPAN, :], accum[slot, 0:QUARTER, :]], axis=0).T

            def part(array, parity):
                return jnp.concatenate(
                    [
                        array[(2 * tile + parity) * rows : (2 * tile + parity + 1) * rows]
                        for tile in range(nwave)
                    ],
                    axis=0,
                )

            edge[slot, rows : rows + total_rows, :] = jnp.where(low_lane, part(far, 1), part(far, 0))
            above = edge[slot, rows - mixes : rows - mixes + total_rows, :]
            below = edge[slot, rows + mixes : rows + mixes + total_rows, :]
            joined = (part(near, 0) + part(near, 1)) + jnp.where(low_lane, above, below)
            for tile in range(nwave):
                send[phase, tile, slot] = joined[tile * rows : (tile + 1) * rows]

    def plane_copy(phase, step):
        other = lax.rem(me_w + step, nwave)
        return pltpu.make_async_remote_copy(
            src_ref=send.at[phase, other],
            dst_ref=recv.at[phase, me_w],
            send_sem=send_sem.at[phase, other],
            recv_sem=recv_sem.at[phase, me_w],
            device_id=(me_s, other),
            device_id_type=MESH,
        )

    def plane_total(phase):
        total = send[phase, me_w]
        for step in range(1, nwave):
            other = lax.rem(me_w + step, nwave)
            pltpu.make_async_remote_copy(
                src_ref=send.at[phase, other],
                dst_ref=recv.at[phase, other],
                send_sem=send_sem.at[phase, other],
                recv_sem=recv_sem.at[phase, other],
                device_id=(me_s, other),
                device_id_type=MESH,
            ).wait_recv()
            total = total + recv[phase, other]
        return total

    def axis_copy(phase):
        group = group_of(phase)
        return pltpu.make_async_remote_copy(
            src_ref=zsend.at[phase],
            dst_ref=zrecv.at[me_s],
            send_sem=zsend_sem.at[phase],
            recv_sem=zrecv_sem.at[me_s],
            device_id=(group, me_w),
            device_id_type=MESH,
        )

    def relay(phase):
        zsend[phase] = plane_total(phase)
        axis_copy(phase).start()

    def spread(phase):
        for step in range(1, nwave):
            plane_copy(phase, step).start()

    def advance(phase, carry):
        evaluate(phase)
        finish(phase)

        @pl.when(phase == 0)
        def _():
            pl.semaphore_wait(barrier, nwave + nspecies - 2)

        spread(phase)

        @pl.when(phase > 0)
        def _():
            relay(phase - 1)

        return carry

    lax.fori_loop(0, nspecies, advance, 0)
    total = plane_total(last)
    for step in range(1, nspecies):
        other = lax.rem(me_s + step, nspecies)
        pltpu.make_async_remote_copy(
            src_ref=zsend.at[0],
            dst_ref=zrecv.at[other],
            send_sem=zsend_sem.at[0],
            recv_sem=zrecv_sem.at[other],
            device_id=(other, me_w),
            device_id_type=MESH,
        ).wait_recv()
        total = total + zrecv[other]
    for mix in range(mixes):
        for half in range(2):
            out[mix, :, half * LANES : (half + 1) * LANES] = total[:, half * mixes + mix, :]
    for phase in range(nspecies):
        for step in range(1, nwave):
            plane_copy(phase, step).wait_send()
    for phase in range(last):
        axis_copy(phase).wait_send()


def per_device(
    dest_tiles,
    line_counts,
    wing_widths,
    species_ids,
    offsets,
    strengths,
    doppler,
    lorentz,
    energy,
    temp_scale,
    press_scale,
    inverse_temp,
    abundances,
):
    nspecies = lax.axis_size("species")
    nwave = lax.axis_size("wave")
    nblocks = dest_tiles.shape[1]
    mixes, _, sub, points = abundances.shape
    chunk = points // nspecies
    rows = 2 * mixes
    total_rows = nwave * rows
    lines = nblocks * LANES
    sizes = (nspecies, nwave, nblocks, points, mixes, sub)
    operands = (
        dest_tiles.reshape(1, nblocks),
        line_counts,
        wing_widths,
        temp_scale,
        press_scale,
        inverse_temp,
        abundances,
        species_ids,
        offsets,
        strengths,
        doppler,
        lorentz,
        energy,
    )
    operands = tuple(pltpu.with_memory_space_constraint(array, pltpu.HBM) for array in operands)
    spaces = [pltpu.SMEM] * 7 + [pltpu.VMEM] * 6
    table = pltpu.VMEM((nblocks, points, LANES), jnp.float32)
    return pl.pallas_call(
        functools.partial(kernel, sizes),
        out_shape=jax.ShapeDtypeStruct((mixes, chunk, 2 * LANES), jnp.float32),
        in_specs=[pl.BlockSpec(memory_space=pltpu.HBM)] * len(operands),
        out_specs=pl.BlockSpec(memory_space=pltpu.VMEM),
        scratch_shapes=[space(array.shape, array.dtype) for space, array in zip(spaces, operands)]
        + [
            pltpu.SemaphoreType.DMA((len(operands),)),
            pltpu.VMEM((WINDOW, lines), jnp.float32),
            table,
            table,
            table,
            pltpu.VMEM((nblocks, points * rows, LANES), jnp.float32),
            pltpu.VMEM((nblocks, STAGES, STEP, LANES), jnp.float32),
            pltpu.VMEM((nblocks, 2 * total_rows, LANES), jnp.bfloat16),
            pltpu.VMEM((mixes, sub, points, LANES), jnp.float32),
            pltpu.VMEM((chunk, SPAN, 2 * total_rows), jnp.float32),
            pltpu.VMEM((chunk, total_rows + 2 * rows, LANES), jnp.float32),
            pltpu.VMEM((nspecies, nwave, chunk, rows, LANES), jnp.float32),
            pltpu.VMEM((nspecies, nwave, chunk, rows, LANES), jnp.float32),
            pltpu.VMEM((nspecies, chunk, rows, LANES), jnp.float32),
            pltpu.VMEM((nspecies, chunk, rows, LANES), jnp.float32),
            pltpu.SemaphoreType.DMA((nspecies, nwave)),
            pltpu.SemaphoreType.DMA((nspecies, nwave)),
            pltpu.SemaphoreType.DMA((nspecies,)),
            pltpu.SemaphoreType.DMA((nspecies,)),
        ],
        compiler_params=pltpu.CompilerParams(collective_id=0, has_side_effects=True, vmem_limit_bytes=24 << 20),
    )(*operands)


def solution(mesh):
    lines = P("species", "wave")
    return jax.shard_map(
        per_device,
        mesh=mesh,
        in_specs=(P("species", "wave", None),)
        + (lines,) * 8
        + (P(), P(), P(), P(None, "species", None, None)),
        out_specs=P(None, "species", "wave"),
        check_vma=False,
    )
```

```python
import functools

import jax
import jax.numpy as jnp
from jax import lax
from jax.experimental import pallas as pl
from jax.experimental.pallas import tpu as pltpu
from jax.sharding import PartitionSpec as P

LANES = 128
HALO = 64
STEP = 16
WINDOW = LANES + STEP
QUARTER = 64
SPAN = QUARTER + 2 * HALO
STAGES = 2
FAR = 1e37
MESH = pl.DeviceIdType.MESH


def column(ref, count):
    rows = lax.broadcasted_iota(jnp.int32, (count, LANES), 0)
    out = jnp.zeros((count, LANES), jnp.float32)
    for index in range(count):
        out = jnp.where(rows == index, ref[index], out)
    return out


def kernel(
    sizes,
    *refs,
):
    nspecies, nwave, nblocks, points, mixes, sub = sizes
    sources, out, scratch = refs[:13], refs[13], refs[14:]
    inputs, input_sem = scratch[:13], scratch[13]
    (
        tiles,
        counts,
        wings,
        temp,
        press,
        inverse,
        abund,
        kinds,
        offsets,
        strengths,
        doppler,
        lorentz,
        energy,
    ) = inputs
    (
        square,
        decay,
        gau_amp,
        table,
        bits,
        route,
        coef,
        accum,
        edge,
        send,
        recv,
        zsend,
        zrecv,
        send_sem,
        recv_sem,
        zsend_sem,
        zrecv_sem,
    ) = scratch[14:]
    chunk = points // nspecies
    last = nspecies - 1
    rows = 2 * mixes
    tile_rows = 2 * rows
    total_rows = nwave * rows
    me_s = lax.axis_index("species")
    me_w = lax.axis_index("wave")

    loads = [
        pltpu.make_async_copy(source, target, input_sem.at[index])
        for index, (source, target) in enumerate(zip(sources, inputs))
    ]
    for load in loads:
        load.start()
    barrier = pltpu.get_barrier_semaphore()
    for step in range(1, nwave):
        pl.semaphore_signal(
            barrier,
            inc=1,
            device_id=(me_s, lax.rem(me_w + step, nwave)),
            device_id_type=MESH,
        )
    for step in range(1, nspecies):
        pl.semaphore_signal(
            barrier,
            inc=1,
            device_id=(lax.rem(me_s + step, nspecies), me_w),
            device_id_type=MESH,
        )

    edge[...] = jnp.zeros(edge.shape, jnp.float32)
    for load in loads[:7]:
        load.wait()
    temp_col = column(temp, points)
    press_col = column(press, points)
    inverse_col = column(inverse, points)
    lane_row = lax.broadcasted_iota(jnp.int32, (1, LANES), 1)
    local = lax.broadcasted_iota(jnp.int32, (WINDOW, LANES), 0).astype(jnp.float32) - HALO
    row_point = lax.broadcasted_iota(jnp.int32, (points, LANES), 0)
    row16 = lax.broadcasted_iota(jnp.int32, (2 * rows, LANES), 0)
    row_quarter = (
        lax.rem(lax.div(row16, mixes), 2) * 2 + lax.div(row16, rows)
    ).astype(jnp.float32)
    for mix in range(mixes):
        for kind in range(sub):
            value = jnp.zeros((points, LANES), jnp.float32)
            for point in range(points):
                value = jnp.where(row_point == point, abund[mix, 0, kind, point], value)
            coef[mix, kind] = value

    for load in loads[7:]:
        load.wait()

    def prepare(block, carry):
        here = pl.ds(pl.multiple_of(block * LANES, LANES), LANES)
        center = offsets[:, here]
        quarter = jnp.clip(jnp.floor(center * (1.0 / QUARTER)), 0.0, 3.0)
        center = center - quarter * float(QUARTER)
        hop = jnp.clip(jnp.floor(center * (1.0 / STEP)), 0.0, float(QUARTER // STEP - 1))
        reach = wings[0, block].astype(jnp.float32)
        offset = local - (center - hop * float(STEP))
        sq = offset * offset
        square[:, here] = jnp.where(sq <= reach * reach, sq, FAR)
        hop_int = hop.astype(jnp.int32)
        for stage in range(STAGES):
            bit = (hop_int >> stage) & 1
            bits[block, stage] = jnp.broadcast_to(bit.astype(jnp.float32), (STEP, LANES))
        gauss = 2.35482 * (temp_col * doppler[:, here])
        lor = 2.0 * (press_col * lorentz[:, here])
        g2 = gauss * gauss
        g4 = g2 * g2
        l2 = lor * lor
        l4 = l2 * l2
        poly = (
            g4 * gauss
            + 2.69269 * g4 * lor
            + 2.42843 * (g2 * gauss) * l2
            + 4.47163 * g2 * (l2 * lor)
            + 0.07842 * gauss * l4
            + l4 * lor
        )
        width = jnp.exp(0.2 * jnp.log(poly))
        inv = 1.0 / width
        ratio = lor * inv
        eta = ratio * (1.36603 + ratio * (-0.47719 + ratio * 0.11116))
        decay[block] = -4.0 * (inv * inv)
        amp_l = eta * inv * (4.0 * 0.15915494)
        amp_g = (1.0 - eta) * inv * 0.9394373
        gau_amp[block] = amp_g / amp_l
        boltz = jnp.exp(-(inverse_col * energy[:, here]))
        strength = jnp.where(lane_row < counts[0, block], strengths[:, here], 0.0)
        kind_row = kinds[:, here]
        for mix in range(mixes):
            mixed = coef[mix, 0]
            for kind in range(1, sub):
                mixed = jnp.where(kind_row == kind, coef[mix, kind], mixed)
            mixed = (mixed * strength) * boltz
            mixed = mixed * amp_l
            for half in range(2):
                table[block, pl.ds(half * mixes + mix, points, stride=rows), :] = mixed
        chosen = jnp.where(row_quarter == quarter, 1.0, 0.0)
        target = tiles[0, block]
        for tile in range(nwave):
            route[block, tile * tile_rows : (tile + 1) * tile_rows, :] = jnp.where(
                target == tile, chosen, 0.0
            ).astype(jnp.bfloat16)
        return carry

    lax.fori_loop(0, nblocks, prepare, 0, unroll=4)

    low_lane = lax.broadcasted_iota(jnp.int32, (total_rows, LANES), 1) < QUARTER
    lane_all = lax.broadcasted_iota(jnp.int32, (LANES, 2 * total_rows), 1)
    odd_lane = lax.rem(lax.div(lane_all, rows), 2) == 1

    def group_of(phase):
        if nspecies % 2:
            return lax.rem(me_s + 1 + phase, nspecies)
        pairs = nspecies // 2
        ahead = pairs - 1 - lax.div(phase, 2)
        other = lax.rem(me_s + 1 + lax.rem(phase, 2), 2)
        return lax.rem(lax.div(me_s, 2) + ahead, pairs) * 2 + other

    def evaluate(phase):
        base = group_of(phase) * chunk
        spots = range(chunk)
        weights = [[] for _ in spots]
        profiles = [[] for _ in spots]

        def one(slot, block):
            point = base + slot
            here = pl.ds(block * LANES, LANES)
            slope = jnp.broadcast_to(decay[block, pl.ds(point, 1), :], (STEP, LANES))
            amp_g = jnp.broadcast_to(gau_amp[block, pl.ds(point, 1), :], (STEP, LANES))
            pieces = []
            for piece in range(WINDOW // STEP):
                sq = square[piece * STEP : (piece + 1) * STEP, here]
                power = sq * slope
                value = 1.0 / (1.0 - power) + amp_g * jnp.exp2(power)
                pieces.append(value.astype(jnp.bfloat16))
            blank = jnp.zeros((STEP, LANES), jnp.bfloat16)
            for stage in range(STAGES):
                hop = 1 << stage
                on = bits[block, stage] > 0
                shifted = [blank] * hop + pieces
                stay = pieces + [blank] * hop
                pieces = [jnp.where(on, a, b) for a, b in zip(shifted, stay)]
            profiles[slot].append(jnp.concatenate(pieces, axis=0))
            weight = table[block, pl.ds(pl.multiple_of(point * rows, rows), rows), :]
            packed = jnp.concatenate([weight, weight], axis=0).astype(jnp.bfloat16)
            weights[slot].append(
                jnp.concatenate(
                    [
                        packed * route[block, tile * tile_rows : (tile + 1) * tile_rows, :]
                        for tile in range(nwave)
                    ],
                    axis=0,
                )
            )

        for slot in spots:
            for block in range(nblocks):
                one(slot, block)
            accum[slot] = lax.dot_general(
                jnp.concatenate(profiles[slot], axis=1),
                jnp.concatenate(weights[slot], axis=1),
                (((1,), (1,)), ((), ())),
                preferred_element_type=jnp.float32,
            )

    def finish(phase):
        for slot in range(chunk):
            near = jnp.where(odd_lane, accum[slot, 0:LANES, :], accum[slot, QUARTER:SPAN, :]).T
            far = jnp.concatenate([accum[slot, LANES:SPAN, :], accum[slot, 0:QUARTER, :]], axis=0).T

            def part(array, parity):
                return jnp.concatenate(
                    [
                        array[(2 * tile + parity) * rows : (2 * tile + parity + 1) * rows]
                        for tile in range(nwave)
                    ],
                    axis=0,
                )

            edge[slot, rows : rows + total_rows, :] = jnp.where(low_lane, part(far, 1), part(far, 0))
            above = edge[slot, rows - mixes : rows - mixes + total_rows, :]
            below = edge[slot, rows + mixes : rows + mixes + total_rows, :]
            joined = (part(near, 0) + part(near, 1)) + jnp.where(low_lane, above, below)
            for tile in range(nwave):
                send[phase, tile, slot] = joined[tile * rows : (tile + 1) * rows]

    def plane_copy(phase, step):
        other = lax.rem(me_w + step, nwave)
        return pltpu.make_async_remote_copy(
            src_ref=send.at[phase, other],
            dst_ref=recv.at[phase, me_w],
            send_sem=send_sem.at[phase, other],
            recv_sem=recv_sem.at[phase, me_w],
            device_id=(me_s, other),
            device_id_type=MESH,
        )

    def plane_total(phase):
        total = send[phase, me_w]
        for step in range(1, nwave):
            other = lax.rem(me_w + step, nwave)
            pltpu.make_async_remote_copy(
                src_ref=send.at[phase, other],
                dst_ref=recv.at[phase, other],
                send_sem=send_sem.at[phase, other],
                recv_sem=recv_sem.at[phase, other],
                device_id=(me_s, other),
                device_id_type=MESH,
            ).wait_recv()
            total = total + recv[phase, other]
        return total

    def axis_copy(phase):
        group = group_of(phase)
        return pltpu.make_async_remote_copy(
            src_ref=zsend.at[phase],
            dst_ref=zrecv.at[me_s],
            send_sem=zsend_sem.at[phase],
            recv_sem=zrecv_sem.at[me_s],
            device_id=(group, me_w),
            device_id_type=MESH,
        )

    def relay(phase):
        zsend[phase] = plane_total(phase)
        axis_copy(phase).start()

    def spread(phase):
        for step in range(1, nwave):
            plane_copy(phase, step).start()

    def advance(phase, carry):
        evaluate(phase)
        finish(phase)

        @pl.when(phase == 0)
        def _():
            pl.semaphore_wait(barrier, nwave + nspecies - 2)

        spread(phase)

        @pl.when(phase > 0)
        def _():
            relay(phase - 1)

        return carry

    lax.fori_loop(0, nspecies, advance, 0)
    total = plane_total(last)
    for step in range(1, nspecies):
        other = lax.rem(me_s + step, nspecies)
        pltpu.make_async_remote_copy(
            src_ref=zsend.at[0],
            dst_ref=zrecv.at[other],
            send_sem=zsend_sem.at[0],
            recv_sem=zrecv_sem.at[other],
            device_id=(other, me_w),
            device_id_type=MESH,
        ).wait_recv()
        total = total + zrecv[other]
    for mix in range(mixes):
        for half in range(2):
            out[mix, :, half * LANES : (half + 1) * LANES] = total[:, half * mixes + mix, :]
    for phase in range(nspecies):
        for step in range(1, nwave):
            plane_copy(phase, step).wait_send()
    for phase in range(last):
        axis_copy(phase).wait_send()


def per_device(
    dest_tiles,
    line_counts,
    wing_widths,
    species_ids,
    offsets,
    strengths,
    doppler,
    lorentz,
    energy,
    temp_scale,
    press_scale,
    inverse_temp,
    abundances,
):
    nspecies = lax.axis_size("species")
    nwave = lax.axis_size("wave")
    nblocks = dest_tiles.shape[1]
    mixes, _, sub, points = abundances.shape
    chunk = points // nspecies
    rows = 2 * mixes
    total_rows = nwave * rows
    lines = nblocks * LANES
    sizes = (nspecies, nwave, nblocks, points, mixes, sub)
    operands = (
        dest_tiles.reshape(1, nblocks),
        line_counts,
        wing_widths,
        temp_scale,
        press_scale,
        inverse_temp,
        abundances,
        species_ids,
        offsets,
        strengths,
        doppler,
        lorentz,
        energy,
    )
    operands = tuple(pltpu.with_memory_space_constraint(array, pltpu.HBM) for array in operands)
    spaces = [pltpu.SMEM] * 7 + [pltpu.VMEM] * 6
    table = pltpu.VMEM((nblocks, points, LANES), jnp.float32)
    return pl.pallas_call(
        functools.partial(kernel, sizes),
        out_shape=jax.ShapeDtypeStruct((mixes, chunk, 2 * LANES), jnp.float32),
        in_specs=[pl.BlockSpec(memory_space=pltpu.HBM)] * len(operands),
        out_specs=pl.BlockSpec(memory_space=pltpu.VMEM),
        scratch_shapes=[space(array.shape, array.dtype) for space, array in zip(spaces, operands)]
        + [
            pltpu.SemaphoreType.DMA((len(operands),)),
            pltpu.VMEM((WINDOW, lines), jnp.float32),
            table,
            table,
            pltpu.VMEM((nblocks, points * rows, LANES), jnp.float32),
            pltpu.VMEM((nblocks, STAGES, STEP, LANES), jnp.float32),
            pltpu.VMEM((nblocks, 2 * total_rows, LANES), jnp.bfloat16),
            pltpu.VMEM((mixes, sub, points, LANES), jnp.float32),
            pltpu.VMEM((chunk, SPAN, 2 * total_rows), jnp.float32),
            pltpu.VMEM((chunk, total_rows + 2 * rows, LANES), jnp.float32),
            pltpu.VMEM((nspecies, nwave, chunk, rows, LANES), jnp.float32),
            pltpu.VMEM((nspecies, nwave, chunk, rows, LANES), jnp.float32),
            pltpu.VMEM((nspecies, chunk, rows, LANES), jnp.float32),
            pltpu.VMEM((nspecies, chunk, rows, LANES), jnp.float32),
            pltpu.SemaphoreType.DMA((nspecies, nwave)),
            pltpu.SemaphoreType.DMA((nspecies, nwave)),
            pltpu.SemaphoreType.DMA((nspecies,)),
            pltpu.SemaphoreType.DMA((nspecies,)),
        ],
        compiler_params=pltpu.CompilerParams(collective_id=0, has_side_effects=True, vmem_limit_bytes=24 << 20),
    )(*operands)


def solution(mesh):
    lines = P("species", "wave")
    return jax.shard_map(
        per_device,
        mesh=mesh,
        in_specs=(P("species", "wave", None),)
        + (lines,) * 8
        + (P(), P(), P(), P(None, "species", None, None)),
        out_specs=P(None, "species", "wave"),
        check_vma=False,
    )
```
